256 devices in a mesh: seq: 32 (over y, x, core), exp: 8 (over z).
Axes of the slice: x: 4, y: 4, z: 8, core: 2. Of those that a mesh axis runs over, the one named last changes fastest.
Arguments:
- mixer_input: bfloat16 [4096, 8192], P('seq', 'exp'), may hold values from -6 to 6
- gate_input: bfloat16 [4096, 8192], P('seq', 'exp'), may hold values from -6 to 6
- delta_raw: bfloat16 [4096, 8192], P('seq', 'exp'), may hold values from -7 to 16387
- input_coef: bfloat16 [4096, 16], P('seq'), may hold values from 0.19921875 to 1.796875
- output_coef: bfloat16 [4096, 16], P('seq'), may hold values from -3 to 3
- decay_rate: float32 [16, 8192], P(None, 'exp'), may hold values from 4.8828125e-06 to 0.05
- conv_weight: float32 [4, 8192], P(None, 'exp'), may hold values from -3 to 3
- conv_bias: float32 [8192], P('exp'), may hold values from -3 to 3
- skip_gain: float32 [8192], P('exp'), may hold values from 0.5 to 1.5
- out_weight: bfloat16 [8192, 4096], P('exp', 'seq'), may hold values from -0.0625 to 0.0625
- residual: bfloat16 [4096, 4096], P(('seq', 'exp')), may hold values from -6 to 6
- norm_gain: float32 [4096], replicated, may hold values from 0.1 to 1.9
- router_weight: bfloat16 [4096, 8], replicated, may hold values from -0.09375 to 0.09375
- expert_ids: int32 [4096, 2], P(('seq', 'exp')), may hold values from 0 to 7, all different within a row; in each aligned block of 16 rows (0 to 15, 16 to 31, ...) at most 5 rows name the same one
- gate_weight: bfloat16 [8, 4096, 12288], P('exp', None, 'seq'), may hold values from -0.09375 to 0.09375
- up_weight: bfloat16 [8, 4096, 12288], P('exp', None, 'seq'), may hold values from -0.09375 to 0.09375
- down_weight: bfloat16 [8, 12288, 4096], P('exp', 'seq'), may hold values from -0.0546875 to 0.0546875
Outputs:
- mixed: bfloat16 [4096, 8192], P('seq', 'exp')
- final: bfloat16 [4096, 4096], P(('seq', 'exp'))
The draws below stay inside these ranges and needn't reach their ends.
Inputs may be any that keep to these rules, and one draw needn't show every extreme that they name: `expert_ids`: each row names two different experts. In each aligned block of 16 rows (the rows of one device) no expert is named by more than 5 rows, and in some block one expert is named by exactly 5 rows.
All inputs are finite; a program needn't handle non-finite values.
Results may differ from the reference program's by a relative error of at most 0.015.
Values may be sent and summed in bfloat16 or wider, within the bound.
No kernel may reach another device: no remote copies, remote signals or barrier semaphores. Data moves between devices by JAX's collectives and lax.ppermute only.
A program may use at most 128 MiB of HBM per device.

```python
import math
import jax
import jax.numpy as jnp
import numpy as np
from jax import lax

D = 4096
INNER = 8192
STATE = 16
KCONV = 4
FF = 12288
ROWS = 16
EXPERTS = 8
SEQ = 4096
CAP = 5
N_SEQ = 32
N_EXP = 8


def draw_delta_raw(key, part):
    base_key = jax.random.fold_in(key, 11)
    spot_key = jax.random.fold_in(key, 12)
    height_key = jax.random.fold_in(key, 13)
    base = jnp.clip(jax.random.normal(base_key, (SEQ, INNER), jnp.float32) - 0.5, -6.5, 3.0)
    spots = jax.random.randint(spot_key, (3,), 0, SEQ)
    heights = jax.random.uniform(height_key, (3,), jnp.float32, 0.5, 2.0) * SEQ
    hits = jnp.arange(SEQ)[:, None] == spots[None, :]
    boost = jnp.sum(jnp.where(hits, heights[None, :], 0.0), axis=1)
    return (base + boost[:, None]).astype(jnp.bfloat16)


def draw_decay_rate(key, part):
    lowest = jnp.float32(0.02) / SEQ
    low = jnp.log(lowest)
    high = jnp.log(jnp.float32(0.05))
    spread_key = jax.random.fold_in(key, 21)
    logs = jax.random.uniform(spread_key, (STATE, INNER), jnp.float32) * (high - low) + low
    return jnp.clip(jnp.exp(logs), lowest, jnp.float32(0.05))


def level_of(key, extent, shards, low, top_value):
    loudness = 1.0
    for dim, shards_of in shards:
        draws = jax.random.uniform(jax.random.fold_in(jax.random.fold_in(key, 6), dim), (shards_of,), jnp.float32, low / len(shards), top_value / len(shards))
        loudness = loudness * jnp.repeat(jnp.exp(draws), extent[dim] // shards_of).reshape((-1,) + (1,) * (len(extent) - 1 - dim))
    return loudness


def shared_out(rng, own, number, rows, count, top, limit, slope):
    order = jax.random.permutation(rng, count)
    heavy_load, common = load_shares(count, rows * top, limit, slope, True), load_shares(count, rows * top, limit, slope, False)
    places = jnp.arange(count)

    def named(lengths, offset_by):
        used = int((lengths > 0).sum())
        fixed = max(1, used // 4)
        moved = fixed + (places - fixed + offset_by * (used - fixed)) % max(1, count - fixed)
        return jnp.zeros((count,), jnp.int32).at[order[jnp.where(places < fixed, places, moved)]].set(jnp.asarray(lengths, jnp.int32))

    lengths = jnp.where(number % 4 == 0, named(heavy_load, number // 4), named(common, number - number // 4 - 1))
    mixed = jax.random.permutation(jax.random.fold_in(own, 3), count)
    donor, taker = mixed[0:count // 2 * 2:2], mixed[1:count // 2 * 2:2]
    margin = jnp.minimum(lengths[donor] - 1, limit - lengths[taker]) // 2
    margin = jnp.where((donor == order[0]) | (taker == order[0]) | (lengths[taker] == 0), 0, jnp.maximum(margin, 0))
    moved = jax.random.randint(jax.random.fold_in(own, 4), (count // 2,), 0, 1 << 20) % (margin + 1)
    lengths = lengths.at[donor].add(-moved).at[taker].add(moved)
    members = jnp.searchsorted(jnp.cumsum(lengths), jnp.arange(rows * top), side="right").astype(jnp.int32)
    grid = members.reshape(top, rows).T
    grid = grid[jax.random.permutation(jax.random.fold_in(own, 1), rows)]
    offset_by = jax.random.randint(jax.random.fold_in(own, 2), (rows, 1), 0, top)
    return jnp.take_along_axis(grid, (jnp.arange(top)[None, :] + offset_by) % top, axis=1)


def load_shares(amount, total, reach, lean, full):
    loads = [(1 << 20) // math.isqrt(rank ** lean) + 1 for rank in range(1, amount + 1)]
    largest = reach if full else min(reach, max(-(-total // amount), total * loads[0] // sum(loads)))
    least = 1 if total - largest >= amount - 1 else 0
    counts, spare = [largest] + [least] * (amount - 1), total - largest - least * (amount - 1)
    while spare > 0:
        free = [i for i in range(1, amount) if counts[i] < largest] or [i for i in range(1, amount) if counts[i] < reach]
        pool, budget = sum([loads[i] for i in free]), spare
        for i in free:
            extra = min(reach - counts[i], max(1, budget * loads[i] // pool), spare)
            counts[i] = counts[i] + extra
            spare = spare - extra
    return np.array(counts)


def gaussian(stream_key, dims, spread, limit, split=(), kind=jnp.bfloat16):
    values = spread * jax.random.normal(stream_key, dims, jnp.float32)
    if split:
        values = values * level_of(stream_key, dims, split, -0.22, 0.18)
    return jnp.clip(values, -limit, limit).astype(kind)


def setup_inputs(seed: int = 0) -> dict:
    arg_keys = jax.random.split(jax.random.key(seed), 18)
    mixer_input = gaussian(arg_keys[0], (SEQ, INNER), 1.0, 6.0, ((0, 32), (1, 8)))
    gate_input = gaussian(arg_keys[1], (SEQ, INNER), 1.0, 6.0, ((0, 32), (1, 8)))
    delta_raw = draw_delta_raw(jax.random.fold_in(arg_keys[17], 71), 0)
    input_coef = jnp.clip(0.19921875 + 1.5976562 * jax.random.uniform(arg_keys[3], (SEQ, STATE), jnp.float32) ** level_of(arg_keys[3], (SEQ, STATE), ((0, 32),), -0.2, 0.2), 0.19921875, 1.796875).astype(jnp.bfloat16)
    output_coef = gaussian(arg_keys[4], (SEQ, STATE), 0.5, 3.0, ((0, 32),))
    decay_rate = draw_decay_rate(jax.random.fold_in(arg_keys[17], 71), 0)
    conv_weight = gaussian(arg_keys[6], (KCONV, INNER), 0.5, 3.0, ((1, 8),), jnp.float32)
    conv_bias = gaussian(arg_keys[7], (INNER,), 0.5, 3.0, ((0, 8),), jnp.float32)
    skip_gain = jnp.clip(0.5 + 1.0 * jax.random.uniform(arg_keys[8], (INNER,), jnp.float32) ** level_of(arg_keys[8], (INNER,), ((0, 8),), -0.2, 0.2), 0.5, 1.5)
    out_weight = gaussian(arg_keys[9], (INNER, D), INNER ** -0.5, 0.0625, ((0, 8), (1, 32)))
    residual = gaussian(arg_keys[10], (SEQ, D), 1.0, 6.0, ((0, 256),))
    norm_gain = jnp.clip(1.0 + 0.18 * jax.random.normal(arg_keys[11], (D,), jnp.float32), 0.1, 1.9)
    router_weight = gaussian(arg_keys[12], (D, EXPERTS), D ** -0.5, 0.09375)
    expert_ids_keys = jax.random.split(jax.random.fold_in(arg_keys[13], 1), SEQ // ROWS)
    expert_ids_turns = jax.random.permutation(jax.random.fold_in(arg_keys[13], 3), SEQ // ROWS)
    expert_ids = jax.vmap(lambda own, number: shared_out(jax.random.fold_in(arg_keys[13], 2), own, number, ROWS, EXPERTS, 2, CAP, 2))(expert_ids_keys, expert_ids_turns).reshape((SEQ, 2))
    gate_weight = gaussian(arg_keys[14], (EXPERTS, D, FF), D ** -0.5, 0.09375, ((0, 8), (2, 32)))
    up_weight = gaussian(arg_keys[15], (EXPERTS, D, FF), D ** -0.5, 0.09375, ((0, 8), (2, 32)))
    down_weight = gaussian(arg_keys[16], (EXPERTS, FF, D), FF ** -0.5, 0.0546875, ((0, 8), (1, 32)))
    return {"mixer_input": mixer_input, "gate_input": gate_input, "delta_raw": delta_raw, "input_coef": input_coef, "output_coef": output_coef, "decay_rate": decay_rate, "conv_weight": conv_weight, "conv_bias": conv_bias, "skip_gain": skip_gain, "out_weight": out_weight, "residual": residual, "norm_gain": norm_gain, "router_weight": router_weight, "expert_ids": expert_ids, "gate_weight": gate_weight, "up_weight": up_weight, "down_weight": down_weight}


def convolve(mixer_input, conv_weight, conv_bias):
    width = mixer_input.shape[1]
    values = mixer_input.astype(jnp.float32)
    length = values.shape[0]
    padded = jnp.concatenate([jnp.zeros((KCONV - 1, width), jnp.float32), values], axis=0)
    summed = jnp.broadcast_to(conv_bias[None, :], (length, width)).astype(jnp.float32)
    for offset in range(KCONV):
        summed = summed + conv_weight[offset][None, :] * padded[offset:offset + length]
    return jax.nn.silu(summed)

def sweep(state, delta, convolved, input_rows, output_rows, decay_rate):

    def advance(carry, inputs):
        delta_row, value_row, input_row, output_row = inputs
        retain = jnp.exp(-delta_row[None, :] * decay_rate)
        carry = retain * carry + (1.0 - retain) * input_row[:, None] * value_row[None, :]
        return (carry, lax.optimization_barrier(jnp.sum(output_row[:, None] * carry, axis=0)))
    return lax.scan(advance, state, (delta, convolved, input_rows, output_rows), unroll=8)

def reference(mixer_input, gate_input, delta_raw, input_coef, output_coef, decay_rate, conv_weight, conv_bias, skip_gain, out_weight, residual, norm_gain, router_weight, expert_ids, gate_weight, up_weight, down_weight):
    convolved = convolve(mixer_input, conv_weight, conv_bias)
    delta = jax.nn.softplus(delta_raw.astype(jnp.float32))
    zero_state = jnp.zeros((STATE, INNER), jnp.float32)
    end_state, scan_out = sweep(zero_state, delta, convolved, input_coef.astype(jnp.float32), output_coef.astype(jnp.float32), decay_rate)
    mixed = ((scan_out + skip_gain[None, :] * convolved) * jax.nn.silu(gate_input.astype(jnp.float32))).astype(jnp.bfloat16)
    block = INNER // N_EXP
    projected = jnp.zeros((SEQ, D), jnp.float32)
    for owner in range(N_EXP):
        term = jnp.dot(mixed[:, owner * block:(owner + 1) * block], out_weight[owner * block:(owner + 1) * block], preferred_element_type=jnp.float32)
        projected = projected + lax.optimization_barrier(term.astype(jnp.bfloat16)).astype(jnp.float32)
    hidden_state = residual.astype(jnp.float32) + projected
    scale = lax.rsqrt(lax.optimization_barrier(jnp.mean(hidden_state * hidden_state, axis=1, keepdims=True)) + 1e-06)
    normed = (hidden_state * scale * norm_gain[None, :]).astype(jnp.bfloat16)
    logits = jnp.dot(normed, router_weight, preferred_element_type=jnp.float32)
    chosen = jnp.take_along_axis(logits, expert_ids, axis=1)
    first = jax.nn.sigmoid(chosen[:, 0] - chosen[:, 1])
    blocks = expert_ids.reshape(-1, 2 * ROWS)
    onehot = (blocks[:, :, None] == jnp.arange(EXPERTS, dtype=jnp.int32)[None, None, :]).astype(jnp.int32)
    before = (jnp.cumsum(onehot, axis=1) - onehot).astype(jnp.int32)
    rank = lax.optimization_barrier(jnp.sum(before * onehot, axis=2)).astype(jnp.int32).reshape(SEQ, 2)
    per_expert = SEQ // ROWS * CAP
    owner_block = (jnp.arange(SEQ, dtype=jnp.int32) // ROWS)[:, None]
    slot_index = (expert_ids * per_expert + owner_block * CAP + rank).astype(jnp.int32).reshape(-1)
    repeated = jnp.broadcast_to(normed[:, None, :], (SEQ, 2, D)).reshape(-1, D)
    buffer = jnp.zeros((EXPERTS * per_expert, D), jnp.bfloat16).at[slot_index].set(repeated).reshape(EXPERTS, per_expert, D)
    hidden_block = FF // N_SEQ

    def serve(operands):
        routed, gate_part, up_part, down_part = operands
        gating = jnp.dot(routed, gate_part, preferred_element_type=jnp.float32)
        upward = jnp.dot(routed, up_part, preferred_element_type=jnp.float32)
        activated = (jax.nn.silu(gating) * upward).astype(jnp.bfloat16)

        def add_block(index, total):
            begin = index * hidden_block
            portion = lax.dynamic_slice_in_dim(activated, begin, hidden_block, 1)
            weights = lax.dynamic_slice_in_dim(down_part, begin, hidden_block, 0)
            term = jnp.dot(portion, weights, preferred_element_type=jnp.float32)
            return total + lax.optimization_barrier(term.astype(jnp.bfloat16)).astype(jnp.float32)
        total = lax.fori_loop(0, N_SEQ, add_block, jnp.zeros((routed.shape[0], D), jnp.float32))
        return total.astype(jnp.bfloat16)
    expert_out = lax.map(serve, (buffer, gate_weight, up_weight, down_weight))
    returned = expert_out.reshape(-1, D)[slot_index].astype(jnp.float32).reshape(SEQ, 2, D)
    moe_out = first[:, None] * returned[:, 0] + (1.0 - first)[:, None] * returned[:, 1]
    final = (hidden_state + moe_out).astype(jnp.bfloat16)
    return (mixed, final)
```

```python
import jax
import jax.numpy as jnp
from jax import lax
from jax.sharding import PartitionSpec as P

KCONV = 4


def from_behind(block, axis, distance):
    devices = range(lax.axis_size(axis))
    route = [(i - distance, i) for i in devices if i - distance in devices]
    return lax.ppermute(block, axis, route)


def carried_in(part, axis, combine, identity):
    place = lax.axis_index(axis)
    gathered = jax.tree.map(lambda a: lax.all_gather(a, axis), part)
    state = jax.tree.map(lambda a, e: jnp.zeros_like(a) + jnp.asarray(e, a.dtype), part, identity)

    def one(turn, state):
        return combine(
            state, jax.tree.map(lambda a: lax.dynamic_index_in_dim(a, turn, 0, False), gathered)
        )

    return lax.fori_loop(0, place, one, state)


def sweep(state, delta, convolved, input_rows, output_rows, decay_rate):

    def advance(carry, inputs):
        delta_row, value_row, input_row, output_row = inputs
        retain = jnp.exp(-delta_row[None, :] * decay_rate)
        carry = retain * carry + (1.0 - retain) * input_row[:, None] * value_row[None, :]
        return (carry, jnp.sum(output_row[:, None] * carry, axis=0))

    return lax.scan(advance, state, (delta, convolved, input_rows, output_rows), unroll=8)


def chain(earlier, later):
    return (earlier[0] * later[0], later[0] * earlier[1] + later[1])


def shards(
    mixer_input,
    gate_input,
    delta_raw,
    input_coef,
    output_coef,
    decay_rate,
    conv_weight,
    conv_bias,
    skip_gain,
    out_weight,
    residual,
    norm_gain,
    router_weight,
    expert_ids,
    gate_weight,
    up_weight,
    down_weight,
):
    length = mixer_input.shape[0]
    width = mixer_input.shape[1]
    tail = mixer_input[length - (KCONV - 1) :]
    before = from_behind(tail, "seq", 1)
    padded = jnp.concatenate([before, mixer_input], axis=0).astype(jnp.float32)
    summed = jnp.broadcast_to(conv_bias[None, :], (length, width))
    for offset in range(KCONV):
        summed = summed + conv_weight[offset][None, :] * padded[offset : offset + length]
    convolved = jax.nn.silu(summed)
    delta = jax.nn.softplus(delta_raw.astype(jnp.float32))
    input_rows = input_coef.astype(jnp.float32)
    output_rows = output_coef.astype(jnp.float32)
    zero_state = jnp.zeros(decay_rate.shape, jnp.float32)
    end_state, local_out = sweep(zero_state, delta, convolved, input_rows, output_rows, decay_rate)
    block_decay = jnp.exp(-jnp.sum(delta, axis=0)[None, :] * decay_rate)
    carried_decay, start_state = carried_in(
        (block_decay, end_state), "seq", chain, (jnp.ones_like(block_decay), zero_state)
    )
    last_state, scan_out = sweep(start_state, delta, convolved, input_rows, output_rows, decay_rate)
    mixed = (
        (scan_out + skip_gain[None, :] * convolved) * jax.nn.silu(gate_input.astype(jnp.float32))
    ).astype(jnp.bfloat16)
    rows = residual.shape[0]
    model_width = residual.shape[1]
    full_weight = lax.all_gather(out_weight, "seq", axis=1, tiled=True)
    projected = lax.psum_scatter(
        jnp.dot(mixed, full_weight, preferred_element_type=jnp.float32).astype(jnp.bfloat16),
        "exp",
        scatter_dimension=0,
        tiled=True,
    ).astype(jnp.float32)
    hidden_state = residual.astype(jnp.float32) + projected
    scale = lax.rsqrt(jnp.mean(hidden_state * hidden_state, axis=1, keepdims=True) + 1e-06)
    normed = (hidden_state * scale * norm_gain[None, :]).astype(jnp.bfloat16)
    experts = router_weight.shape[1]
    capacity = 2 * rows // experts + 1
    logits = jnp.dot(normed, router_weight, preferred_element_type=jnp.float32)
    expert_range = jnp.arange(experts, dtype=jnp.int32)
    matches = expert_ids[:, :, None] == expert_range[None, None, :]
    chosen = jnp.sum(jnp.where(matches, logits[:, None, :], 0.0), axis=2)
    first = jax.nn.sigmoid(chosen[:, 0] - chosen[:, 1])
    flat_ids = expert_ids.reshape(-1)
    position = jnp.arange(flat_ids.shape[0], dtype=jnp.int32)
    earlier = (flat_ids[:, None] == flat_ids[None, :]) & (position[None, :] < position[:, None])
    rank = jnp.sum(earlier.astype(jnp.int32), axis=1)
    target = flat_ids * capacity + rank
    placing = (jnp.arange(experts * capacity, dtype=jnp.int32)[:, None] == target[None, :]).astype(
        jnp.bfloat16
    )
    repeated = jnp.broadcast_to(normed[:, None, :], (rows, 2, model_width)).reshape(-1, model_width)
    outgoing = (
        jnp.dot(placing, repeated, preferred_element_type=jnp.float32)
        .astype(jnp.bfloat16)
        .reshape(experts, capacity, model_width)
    )
    arrived = lax.all_to_all(outgoing, "exp", split_axis=0, concat_axis=0, tiled=True)
    flat_rows = arrived.reshape(-1, arrived.shape[2])
    piece = lax.all_gather(flat_rows, "seq", axis=0, tiled=True)
    gating = jnp.dot(piece, gate_weight[0], preferred_element_type=jnp.float32)
    upward = jnp.dot(piece, up_weight[0], preferred_element_type=jnp.float32)
    activated = (jax.nn.silu(gating) * upward).astype(jnp.bfloat16)
    partial_out = jnp.dot(activated, down_weight[0], preferred_element_type=jnp.float32)
    summed_out = lax.psum_scatter(
        partial_out.astype(jnp.bfloat16), "seq", scatter_dimension=0, tiled=True
    )
    returned = lax.all_to_all(
        summed_out.reshape(arrived.shape), "exp", split_axis=0, concat_axis=0, tiled=True
    )
    flat_returned = returned.reshape(-1, model_width)
    picked = jnp.einsum(
        "sa,sd->ad", placing, flat_returned, preferred_element_type=jnp.float32
    ).reshape(rows, 2, model_width)
    moe_out = first[:, None] * picked[:, 0] + (1.0 - first)[:, None] * picked[:, 1]
    final = (hidden_state + moe_out).astype(jnp.bfloat16)
    return (mixed, final)


def solution(mesh):
    return jax.shard_map(
        shards,
        mesh=mesh,
        in_specs=(
            P("seq", "exp"),
            P("seq", "exp"),
            P("seq", "exp"),
            P("seq", None),
            P("seq", None),
            P(None, "exp"),
            P(None, "exp"),
            P("exp"),
            P("exp"),
            P("exp", "seq"),
            P(("seq", "exp"), None),
            P(),
            P(),
            P(("seq", "exp"), None),
            P("exp", None, "seq"),
            P("exp", None, "seq"),
            P("exp", "seq", None),
        ),
        out_specs=(P("seq", "exp"), P(("seq", "exp"), None)),
        check_vma=False,
    )
```

```python
import functools
import math

import jax
import jax.numpy as jnp
from jax import lax
from jax.experimental import pallas as pl
from jax.experimental.pallas import tpu as pltpu
from jax.sharding import PartitionSpec as P

KCONV = 4
LANES = 128
SUB = 8
CORES = 2
SIDE = 4
LOG2E = math.log2(math.e)
VMEM = pl.BlockSpec(memory_space=pltpu.VMEM)
SMEM = pl.BlockSpec(memory_space=pltpu.SMEM)


def split_place(place):
    return place // (SIDE * CORES), (place // CORES) % SIDE, place % CORES


def join_place(y, x, c):
    return (y % SIDE * SIDE + x % SIDE) * CORES + c % CORES


def moved(block, dy=0, dx=0, dc=0):
    route = []
    for i in range(SIDE * SIDE * CORES):
        y, x, c = split_place(i)
        route.append((i, join_place(y + dy, x + dx, c + dc)))
    return lax.ppermute(block, "seq", route)


def local_scan_kernel(
    inp_ref, before_ref, raw_ref, rate_ref, taps_ref, bias_ref, skip_ref, in_ref, out_ref,
    y_ref, sums_ref, carry_ref, scaled_ref,
    pad_ref, delta_ref, conv_ref,
):
    length, width = inp_ref.shape
    states = rate_ref.shape[0]
    tiles = width // LANES
    for j in range(tiles):
        cols = slice(j * LANES, (j + 1) * LANES)
        pad_ref[SUB - KCONV + 1 : SUB, :] = before_ref[:, cols].astype(jnp.float32)
        pad_ref[SUB:, :] = inp_ref[:, cols].astype(jnp.float32)
        summed = jnp.broadcast_to(bias_ref[:, cols], (length, LANES))
        for k in range(KCONV):
            begin = SUB - KCONV + 1 + k
            summed = summed + taps_ref[k : k + 1, cols] * pad_ref[begin : begin + length, :]
        conv_ref[pl.ds(j, length, stride=tiles), :] = summed * jax.nn.sigmoid(summed)
        raw = raw_ref[:, cols].astype(jnp.float32)
        delta_ref[pl.ds(j, length, stride=tiles), :] = jnp.maximum(raw, 0.0) + jnp.log1p(
            jnp.exp(-jnp.abs(raw))
        )
        scaled_ref[pl.ds(j, states, stride=tiles), :] = rate_ref[:, cols] * -LOG2E

    skip = skip_ref[...]

    def step(t, carry):
        total, state = carry
        rows = pl.ds(pl.multiple_of(t * SUB, SUB), SUB)
        delta, value = delta_ref[rows, :], conv_ref[rows, :]
        total = total + delta
        out = skip * value
        after = []
        for n in range(states):
            retain = jnp.exp2(delta * scaled_ref[n * SUB : (n + 1) * SUB, :])
            fresh = in_ref[t * states + n] * value
            now = fresh + retain * (state[n] - fresh)
            out = out + out_ref[t * states + n] * now
            after.append(now)
        sums_ref[rows, :] = total
        y_ref[rows, :] = out
        return total, tuple(after)

    zero = jnp.zeros((SUB, LANES), jnp.float32)
    total, state = lax.fori_loop(0, length, step, (zero, (zero,) * states), unroll=2)
    for n in range(states):
        carry_ref[n * SUB : (n + 1) * SUB, :] = state[n]
    carry_ref[states * SUB :, :] = total


def finish_scan_kernel(y_ref, sums_ref, start_ref, scaled_ref, gate_ref, out_ref, mixed_ref, full_ref):
    length, width = gate_ref.shape
    states = start_ref.shape[0] // SUB
    tiles = width // LANES

    def step(t, carry):
        rows = pl.ds(pl.multiple_of(t * SUB, SUB), SUB)
        total, out = sums_ref[rows, :], y_ref[rows, :]
        for n in range(states):
            part = slice(n * SUB, (n + 1) * SUB)
            kept = jnp.exp2(total * scaled_ref[part, :]) * start_ref[part, :]
            out = out + out_ref[t * states + n] * kept
        full_ref[rows, :] = out
        return carry

    lax.fori_loop(0, length, step, 0, unroll=2)
    for j in range(tiles):
        cols = slice(j * LANES, (j + 1) * LANES)
        gate = gate_ref[:, cols].astype(jnp.float32)
        gated = full_ref[pl.ds(j, length, stride=tiles), :] * (gate * jax.nn.sigmoid(gate))
        mixed_ref[:, cols] = gated.astype(mixed_ref.dtype)


def local_scan(inp, before, raw, rate, taps, bias, skip, in_flat, out_flat):
    length, width = inp.shape
    states = rate.shape[0]
    flat = jax.ShapeDtypeStruct((length * SUB, LANES), jnp.float32)
    return pl.pallas_call(
        local_scan_kernel,
        name="local_scan",
        out_shape=(
            flat,
            flat,
            jax.ShapeDtypeStruct(((states + 1) * SUB, LANES), jnp.float32),
            jax.ShapeDtypeStruct((states * SUB, LANES), jnp.float32),
        ),
        in_specs=[VMEM] * 7 + [SMEM] * 2,
        out_specs=(VMEM,) * 4,
        scratch_shapes=[
            pltpu.VMEM((length + SUB, LANES), jnp.float32),
            pltpu.VMEM((length * SUB, LANES), jnp.float32),
            pltpu.VMEM((length * SUB, LANES), jnp.float32),
        ],
        compiler_params=pltpu.CompilerParams(vmem_limit_bytes=24 << 20),
        cost_estimate=pl.CostEstimate(flops=8_000_000, transcendentals=2_500_000, bytes_accessed=2_000_000),
    )(inp, before, raw, rate, taps, bias, skip, in_flat, out_flat)


def finish_scan(y, sums, start, scaled, gate, out_flat):
    length, width = gate.shape
    return pl.pallas_call(
        finish_scan_kernel,
        name="finish_scan",
        out_shape=jax.ShapeDtypeStruct((length, width), jnp.bfloat16),
        in_specs=[VMEM] * 5 + [SMEM],
        out_specs=VMEM,
        scratch_shapes=[pltpu.VMEM((length * SUB, LANES), jnp.float32)],
        compiler_params=pltpu.CompilerParams(vmem_limit_bytes=24 << 20),
        cost_estimate=pl.CostEstimate(flops=8_000_000, transcendentals=2_500_000, bytes_accessed=2_000_000),
    )(y, sums, start, scaled, gate, out_flat)


def entering_state(carry, scaled):
    states = scaled.shape[0] // SUB
    scaled = scaled.reshape(states, SUB, LANES)
    y, x, c = split_place(lax.axis_index("seq"))

    def parts(block):
        block = block.reshape(states + 1, SUB, LANES)
        return block[states], block[:states]

    def kept(span, state):
        return jnp.exp2(span[None] * scaled) * state

    def packed(span, state):
        return jnp.concatenate([state, span[None]], axis=0).reshape(carry.shape)

    own = parts(carry)
    other = parts(moved(carry, dc=1))
    is_first = c == 0
    first = [jnp.where(is_first, a, b) for a, b in zip(own, other)]
    last = [jnp.where(is_first, b, a) for a, b in zip(own, other)]
    chip = (first[0] + last[0], kept(last[0], first[1]) + last[1])
    start = jnp.where(is_first, 0.0, other[1])
    span = jnp.where(is_first, 0.0, other[0])

    sent = packed(*chip)
    near = [parts(moved(sent, dx=k)) for k in range(1, SIDE)]
    ahead = jnp.zeros_like(span)
    behind = jnp.zeros_like(span)
    row_state = jnp.zeros_like(chip[1])
    earlier_state = jnp.zeros_like(chip[1])
    for k in range(1, SIDE):
        got_span, got_state = near[k - 1]
        is_earlier = k <= x
        earlier_state = earlier_state + jnp.where(is_earlier, kept(ahead, got_state), 0.0)
        row_state = row_state + jnp.where(is_earlier, 0.0, kept(behind, got_state))
        ahead = ahead + jnp.where(is_earlier, got_span, 0.0)
        behind = behind + jnp.where(is_earlier, 0.0, got_span)
    row_state = row_state + kept(behind, chip[1] + kept(chip[0], earlier_state))
    row_span = ahead + chip[0] + behind
    start = start + kept(span, earlier_state)
    span = span + ahead

    sent = packed(row_span, row_state)
    far = [parts(moved(sent, dy=k)) for k in range(1, SIDE)]
    for k in range(1, SIDE):
        got_span, got_state = far[k - 1]
        is_earlier = k <= y
        start = start + jnp.where(is_earlier, kept(span, got_state), 0.0)
        span = span + jnp.where(is_earlier, got_span, 0.0)
    return start.reshape(states * SUB, LANES)


def from_before(tail):
    count = lax.axis_size("seq")
    return lax.ppermute(tail, "seq", [(i, i + 1) for i in range(count - 1)])


def shards(
    mixer_input,
    gate_input,
    delta_raw,
    input_coef,
    output_coef,
    decay_rate,
    conv_weight,
    conv_bias,
    skip_gain,
    out_weight,
    residual,
    norm_gain,
    router_weight,
    expert_ids,
    gate_weight,
    up_weight,
    down_weight,
):
    length = mixer_input.shape[0]
    in_flat = input_coef.astype(jnp.float32).reshape(-1)
    out_flat = output_coef.astype(jnp.float32).reshape(-1)
    before = from_before(mixer_input[length - (KCONV - 1) :])
    y, sums, carry, scaled = local_scan(
        mixer_input,
        before,
        delta_raw,
        decay_rate,
        conv_weight,
        conv_bias.reshape(1, -1),
        skip_gain.reshape(SUB, LANES),
        in_flat,
        out_flat,
    )
    start = entering_state(carry, scaled)
    mixed = finish_scan(y, sums, start, scaled, gate_input, out_flat)
    rows = residual.shape[0]
    model_width = residual.shape[1]
    full_weight = lax.all_gather(out_weight, "seq", axis=1, tiled=True)
    projected = lax.psum_scatter(
        jnp.dot(mixed, full_weight, preferred_element_type=jnp.float32).astype(jnp.bfloat16),
        "exp",
        scatter_dimension=0,
        tiled=True,
    ).astype(jnp.float32)
    hidden_state = residual.astype(jnp.float32) + projected
    scale = lax.rsqrt(jnp.mean(hidden_state * hidden_state, axis=1, keepdims=True) + 1e-06)
    normed = (hidden_state * scale * norm_gain[None, :]).astype(jnp.bfloat16)
    experts = router_weight.shape[1]
    capacity = 2 * rows // experts + 1
    logits = jnp.dot(normed, router_weight, preferred_element_type=jnp.float32)
    expert_range = jnp.arange(experts, dtype=jnp.int32)
    matches = expert_ids[:, :, None] == expert_range[None, None, :]
    chosen = jnp.sum(jnp.where(matches, logits[:, None, :], 0.0), axis=2)
    first = jax.nn.sigmoid(chosen[:, 0] - chosen[:, 1])
    flat_ids = expert_ids.reshape(-1)
    position = jnp.arange(flat_ids.shape[0], dtype=jnp.int32)
    earlier = (flat_ids[:, None] == flat_ids[None, :]) & (position[None, :] < position[:, None])
    rank = jnp.sum(earlier.astype(jnp.int32), axis=1)
    target = flat_ids * capacity + rank
    placing = (jnp.arange(experts * capacity, dtype=jnp.int32)[:, None] == target[None, :]).astype(
        jnp.bfloat16
    )
    repeated = jnp.broadcast_to(normed[:, None, :], (rows, 2, model_width)).reshape(-1, model_width)
    outgoing = (
        jnp.dot(placing, repeated, preferred_element_type=jnp.float32)
        .astype(jnp.bfloat16)
        .reshape(experts, capacity, model_width)
    )
    arrived = lax.all_to_all(outgoing, "exp", split_axis=0, concat_axis=0, tiled=True)
    flat_rows = arrived.reshape(-1, arrived.shape[2])
    piece = lax.all_gather(flat_rows, "seq", axis=0, tiled=True)
    gating = jnp.dot(piece, gate_weight[0], preferred_element_type=jnp.float32)
    upward = jnp.dot(piece, up_weight[0], preferred_element_type=jnp.float32)
    activated = (jax.nn.silu(gating) * upward).astype(jnp.bfloat16)
    partial_out = jnp.dot(activated, down_weight[0], preferred_element_type=jnp.float32)
    summed_out = lax.psum_scatter(
        partial_out.astype(jnp.bfloat16), "seq", scatter_dimension=0, tiled=True
    )
    returned = lax.all_to_all(
        summed_out.reshape(arrived.shape), "exp", split_axis=0, concat_axis=0, tiled=True
    )
    flat_returned = returned.reshape(-1, model_width)
    picked = jnp.einsum(
        "sa,sd->ad", placing, flat_returned, preferred_element_type=jnp.float32
    ).reshape(rows, 2, model_width)
    moe_out = first[:, None] * picked[:, 0] + (1.0 - first)[:, None] * picked[:, 1]
    final = (hidden_state + moe_out).astype(jnp.bfloat16)
    return (mixed, final)


def solution(mesh):
    return jax.shard_map(
        shards,
        mesh=mesh,
        in_specs=(
            P("seq", "exp"),
            P("seq", "exp"),
            P("seq", "exp"),
            P("seq", None),
            P("seq", None),
            P(None, "exp"),
            P(None, "exp"),
            P("exp"),
            P("exp"),
            P("exp", "seq"),
            P(("seq", "exp"), None),
            P(),
            P(),
            P(("seq", "exp"), None),
            P("exp", None, "seq"),
            P("exp", None, "seq"),
            P("exp", "seq", None),
        ),
        out_specs=(P("seq", "exp"), P(("seq", "exp"), None)),
        check_vma=False,
    )
```

```python
import functools
import math

import jax
import jax.numpy as jnp
from jax import lax
from jax.experimental import pallas as pl
from jax.experimental.pallas import tpu as pltpu
from jax.sharding import PartitionSpec as P

KCONV = 4
LANES = 128
SUB = 8
CORES = 2
SIDE = 4
LOG2E = math.log2(math.e)
VMEM = pl.BlockSpec(memory_space=pltpu.VMEM)
SMEM = pl.BlockSpec(memory_space=pltpu.SMEM)


def split_place(place):
    return place // (SIDE * CORES), (place // CORES) % SIDE, place % CORES


def join_place(y, x, c):
    return (y % SIDE * SIDE + x % SIDE) * CORES + c % CORES


def moved(block, dy=0, dx=0, dc=0):
    route = []
    for i in range(SIDE * SIDE * CORES):
        y, x, c = split_place(i)
        route.append((i, join_place(y + dy, x + dx, c + dc)))
    return lax.ppermute(block, "seq", route)


def local_scan_kernel(
    inp_ref, before_ref, raw_ref, rate_ref, taps_ref, bias_ref, skip_ref, in_ref, out_ref,
    y_ref, sums_ref, carry_ref, scaled_ref,
    pad_ref, delta_ref, conv_ref,
):
    length, width = inp_ref.shape
    states = rate_ref.shape[0]
    tiles = width // LANES
    for j in range(tiles):
        cols = slice(j * LANES, (j + 1) * LANES)
        pad_ref[SUB - KCONV + 1 : SUB, :] = before_ref[:, cols].astype(jnp.float32)
        pad_ref[SUB:, :] = inp_ref[:, cols].astype(jnp.float32)
        summed = jnp.broadcast_to(bias_ref[:, cols], (length, LANES))
        for k in range(KCONV):
            begin = SUB - KCONV + 1 + k
            summed = summed + taps_ref[k : k + 1, cols] * pad_ref[begin : begin + length, :]
        conv_ref[pl.ds(j, length, stride=tiles), :] = summed * jax.nn.sigmoid(summed)
        raw = raw_ref[:, cols].astype(jnp.float32)
        delta_ref[pl.ds(j, length, stride=tiles), :] = jnp.maximum(raw, 0.0) + jnp.log1p(
            jnp.exp(-jnp.abs(raw))
        )
        scaled_ref[pl.ds(j, states, stride=tiles), :] = rate_ref[:, cols] * -LOG2E

    skip = skip_ref[...]

    def step(t, carry):
        total, state = carry
        rows = pl.ds(pl.multiple_of(t * SUB, SUB), SUB)
        delta, value = delta_ref[rows, :], conv_ref[rows, :]
        total = total + delta
        out = skip * value
        after = []
        for n in range(states):
            retain = jnp.exp2(delta * scaled_ref[n * SUB : (n + 1) * SUB, :])
            fresh = in_ref[t * states + n] * value
            now = fresh + retain * (state[n] - fresh)
            out = out + out_ref[t * states + n] * now
            after.append(now)
        sums_ref[rows, :] = total
        y_ref[rows, :] = out
        return total, tuple(after)

    zero = jnp.zeros((SUB, LANES), jnp.float32)
    total, state = lax.fori_loop(0, length, step, (zero, (zero,) * states), unroll=2)
    for n in range(states):
        carry_ref[n * SUB : (n + 1) * SUB, :] = state[n]
    carry_ref[states * SUB :, :] = total


def finish_scan_kernel(y_ref, sums_ref, start_ref, scaled_ref, gate_ref, out_ref, mixed_ref, full_ref):
    length, width = gate_ref.shape
    states = start_ref.shape[0] // SUB
    tiles = width // LANES

    def step(t, carry):
        rows = pl.ds(pl.multiple_of(t * SUB, SUB), SUB)
        total, out = sums_ref[rows, :], y_ref[rows, :]
        for n in range(states):
            part = slice(n * SUB, (n + 1) * SUB)
            kept = jnp.exp2(total * scaled_ref[part, :]) * start_ref[part, :]
            out = out + out_ref[t * states + n] * kept
        full_ref[rows, :] = out
        return carry

    lax.fori_loop(0, length, step, 0, unroll=2)
    for j in range(tiles):
        cols = slice(j * LANES, (j + 1) * LANES)
        gate = gate_ref[:, cols].astype(jnp.float32)
        gated = full_ref[pl.ds(j, length, stride=tiles), :] * (gate * jax.nn.sigmoid(gate))
        mixed_ref[:, cols] = gated.astype(mixed_ref.dtype)


def local_scan(inp, before, raw, rate, taps, bias, skip, in_flat, out_flat):
    length, width = inp.shape
    states = rate.shape[0]
    flat = jax.ShapeDtypeStruct((length * SUB, LANES), jnp.float32)
    return pl.pallas_call(
        local_scan_kernel,
        name="local_scan",
        out_shape=(
            flat,
            flat,
            jax.ShapeDtypeStruct(((states + 1) * SUB, LANES), jnp.float32),
            jax.ShapeDtypeStruct((states * SUB, LANES), jnp.float32),
        ),
        in_specs=[VMEM] * 7 + [SMEM] * 2,
        out_specs=(VMEM,) * 4,
        scratch_shapes=[
            pltpu.VMEM((length + SUB, LANES), jnp.float32),
            pltpu.VMEM((length * SUB, LANES), jnp.float32),
            pltpu.VMEM((length * SUB, LANES), jnp.float32),
        ],
        compiler_params=pltpu.CompilerParams(vmem_limit_bytes=24 << 20),
        cost_estimate=pl.CostEstimate(flops=8_000_000, transcendentals=2_500_000, bytes_accessed=2_000_000),
    )(inp, before, raw, rate, taps, bias, skip, in_flat, out_flat)


def finish_scan(y, sums, start, scaled, gate, out_flat):
    length, width = gate.shape
    return pl.pallas_call(
        finish_scan_kernel,
        name="finish_scan",
        out_shape=jax.ShapeDtypeStruct((length, width), jnp.bfloat16),
        in_specs=[VMEM] * 5 + [SMEM],
        out_specs=VMEM,
        scratch_shapes=[pltpu.VMEM((length * SUB, LANES), jnp.float32)],
        compiler_params=pltpu.CompilerParams(vmem_limit_bytes=24 << 20),
        cost_estimate=pl.CostEstimate(flops=8_000_000, transcendentals=2_500_000, bytes_accessed=2_000_000),
    )(y, sums, start, scaled, gate, out_flat)


def entering_state(carry, scaled):
    states = scaled.shape[0] // SUB
    scaled = scaled.reshape(states, SUB, LANES)
    y, x, c = split_place(lax.axis_index("seq"))

    def parts(block):
        block = block.reshape(states + 1, SUB, LANES)
        return block[states], block[:states]

    def kept(span, state):
        return jnp.exp2(span[None] * scaled) * state

    def packed(span, state):
        return jnp.concatenate([state, span[None]], axis=0).reshape(carry.shape)

    own = parts(carry)
    other = parts(moved(carry, dc=1))
    is_first = c == 0
    first = [jnp.where(is_first, a, b) for a, b in zip(own, other)]
    last = [jnp.where(is_first, b, a) for a, b in zip(own, other)]
    chip = (first[0] + last[0], kept(last[0], first[1]) + last[1])
    start = jnp.where(is_first, 0.0, other[1])
    span = jnp.where(is_first, 0.0, other[0])

    sent = packed(*chip)
    near = [parts(moved(sent, dx=k)) for k in range(1, SIDE)]
    ahead = jnp.zeros_like(span)
    behind = jnp.zeros_like(span)
    row_state = jnp.zeros_like(chip[1])
    earlier_state = jnp.zeros_like(chip[1])
    for k in range(1, SIDE):
        got_span, got_state = near[k - 1]
        is_earlier = k <= x
        earlier_state = earlier_state + jnp.where(is_earlier, kept(ahead, got_state), 0.0)
        row_state = row_state + jnp.where(is_earlier, 0.0, kept(behind, got_state))
        ahead = ahead + jnp.where(is_earlier, got_span, 0.0)
        behind = behind + jnp.where(is_earlier, 0.0, got_span)
    row_state = row_state + kept(behind, chip[1] + kept(chip[0], earlier_state))
    row_span = ahead + chip[0] + behind
    start = start + kept(span, earlier_state)
    span = span + ahead

    sent = packed(row_span, row_state)
    far = [parts(moved(sent, dy=k)) for k in range(1, SIDE)]
    for k in range(1, SIDE):
        got_span, got_state = far[k - 1]
        is_earlier = k <= y
        start = start + jnp.where(is_earlier, kept(span, got_state), 0.0)
        span = span + jnp.where(is_earlier, got_span, 0.0)
    return start.reshape(states * SUB, LANES)


def from_before(tail):
    count = lax.axis_size("seq")
    return lax.ppermute(tail, "seq", [(i, i + 1) for i in range(count - 1)])


def around(block, along, step):
    return moved(block, dy=step) if along == "y" else moved(block, dx=step)


def gather_rows(block, inner, outer):
    near = [block] + [around(block, inner, k) for k in range(1, SIDE)]
    low, high = jnp.concatenate(near[:2], axis=0), jnp.concatenate(near[2:], axis=0)
    low_up = around(low, outer, 1)
    high_down = around(high, outer, -1)
    high_up = around(high, outer, 1)
    low_down = around(low, outer, -1)
    low_far = around(low_up, outer, 1)
    high_far = around(high_down, outer, -1)
    return (low, high), (low_up, high_up), (low_far, high_far), (low_down, high_down)


def added(*terms):
    return sum(t.astype(jnp.float32) for t in terms)


def scatter_sums(groups, inner, outer):
    (low, high), (low_up, high_up), (low_far, high_far), (low_down, high_down) = groups
    dtype = low.dtype
    low_relay = around(low_far, outer, 1)
    high_relay = around(high_far, outer, -1)
    got_high_down = around(high_down, outer, 1)
    got_low_up = around(low_up, outer, -1)
    got_low_down = around(added(low_down, low_relay).astype(dtype), outer, 1)
    got_high_up = around(added(high_up, high_relay).astype(dtype), outer, -1)
    low_sum = added(low, got_low_down, got_low_up)
    high_sum = added(high, got_high_down, got_high_up)
    rows = low.shape[0] // 2
    blocks = [low_sum[:rows], low_sum[rows:], high_sum[:rows], high_sum[rows:]]
    near = [around(blocks[k].astype(dtype), inner, -k) for k in range(1, SIDE)]
    return added(blocks[0], *near).astype(dtype)


def expert_in_kernel(*refs):
    pieces, (gate_a, gate_b, up_a, up_b, act_a, act_b, rows_ref) = refs[:16], refs[16:]
    half, width = pieces[0].shape
    rows = half // 2

    @pl.when(pl.program_id(0) == 0)
    def _():
        for k in range(SIDE):
            for h in range(2):
                begin = (2 * k + h) * half
                rows_ref[begin : begin + half, :width] = pieces[2 * k + h][...]
                for i in range(2):
                    begin = ((2 * h + i) * SIDE + k) * rows
                    block = pieces[8 + 2 * k + h][i * rows : (i + 1) * rows, :]
                    rows_ref[begin : begin + rows, width:] = block

    for gate, up, act in ((gate_a, up_a, act_a), (gate_b, up_b, act_b)):
        both = jnp.concatenate([gate[...], up[...]], axis=1)
        hidden = jnp.dot(rows_ref[...], both, preferred_element_type=jnp.float32)
        gating, upward = hidden[:, :LANES], hidden[:, LANES:]
        act[...] = (gating * jax.nn.sigmoid(gating) * upward).astype(act.dtype)


def expert_in(pieces, gate_a, gate_b, up_a, up_b):
    half, width = pieces[0].shape
    count = 2 * SIDE * half
    hidden = gate_a.shape[1]
    weight = pl.BlockSpec((2 * width, LANES), lambda i: (0, i))
    act = pl.BlockSpec((count, LANES), lambda i: (0, i))
    out = jax.ShapeDtypeStruct((count, hidden), jnp.bfloat16)
    return pl.pallas_call(
        expert_in_kernel,
        name="expert_in",
        grid=(hidden // LANES,),
        out_shape=(out, out),
        in_specs=[VMEM] * 16 + [weight] * 4,
        out_specs=(act, act),
        scratch_shapes=[pltpu.VMEM((count, 2 * width), jnp.bfloat16)],
        compiler_params=pltpu.CompilerParams(vmem_limit_bytes=48 << 20),
        cost_estimate=pl.CostEstimate(
            flops=8 * count * width * hidden * 2, transcendentals=2 * count * hidden, bytes_accessed=20_000_000
        ),
    )(*pieces, gate_a, gate_b, up_a, up_b)


def expert_out_kernel(by_outer, act_a, act_b, down_a, down_b, *outs):
    half = outs[0].shape[0]
    rows = half // 2
    acts = jnp.concatenate([act_a[...], act_b[...]], axis=1)
    down = jnp.concatenate([down_a[...], down_b[...]], axis=0)
    result = jnp.dot(acts, down, preferred_element_type=jnp.float32).astype(outs[0].dtype)
    for k in range(SIDE):
        for h in range(2):
            if by_outer:
                begin = (2 * k + h) * half
                outs[2 * k + h][...] = result[begin : begin + half]
            else:
                for i in range(2):
                    begin = ((2 * h + i) * SIDE + k) * rows
                    outs[2 * k + h][i * rows : (i + 1) * rows, :] = result[begin : begin + rows]


def expert_out(by_outer, act_a, act_b, down_a, down_b):
    count, hidden = act_a.shape
    width = down_a.shape[1] // 2
    tile = 4 * LANES
    tiles = width // tile
    skip = 0 if by_outer else tiles
    half = count // (2 * SIDE)
    weight = pl.BlockSpec((hidden, tile), lambda i: (0, i + skip))
    piece = pl.BlockSpec((half, tile), lambda i: (0, i))
    out = jax.ShapeDtypeStruct((half, width), jnp.bfloat16)
    outs = pl.pallas_call(
        functools.partial(expert_out_kernel, by_outer),
        name="expert_out",
        grid=(tiles,),
        out_shape=(out,) * 8,
        in_specs=[VMEM] * 2 + [weight] * 2,
        out_specs=(piece,) * 8,
        compiler_params=pltpu.CompilerParams(vmem_limit_bytes=32 << 20),
        cost_estimate=pl.CostEstimate(
            flops=4 * count * width * hidden, transcendentals=0, bytes_accessed=8_000_000
        ),
    )(act_a, act_b, down_a, down_b)
    return [outs[2 * k : 2 * k + 2] for k in range(SIDE)]


def experts_of_rows(rows, gate, up, down):
    other_gate, other_up, other_down = (moved(w, dc=1) for w in (gate, up, down))
    width = rows.shape[1] // 2
    first = gather_rows(rows[:, :width], "x", "y")
    second = gather_rows(rows[:, width:], "y", "x")
    pieces = [p for groups in (first, second) for pair in groups for p in pair]
    act, other_act = expert_in(pieces, gate, other_gate, up, other_up)
    first = expert_out(True, act, other_act, down, other_down)
    second = expert_out(False, act, other_act, down, other_down)
    return jnp.concatenate(
        [scatter_sums(first, "x", "y"), scatter_sums(second, "y", "x")], axis=1
    )


def shards(
    mixer_input,
    gate_input,
    delta_raw,
    input_coef,
    output_coef,
    decay_rate,
    conv_weight,
    conv_bias,
    skip_gain,
    out_weight,
    residual,
    norm_gain,
    router_weight,
    expert_ids,
    gate_weight,
    up_weight,
    down_weight,
):
    length = mixer_input.shape[0]
    in_flat = input_coef.astype(jnp.float32).reshape(-1)
    out_flat = output_coef.astype(jnp.float32).reshape(-1)
    before = from_before(mixer_input[length - (KCONV - 1) :])
    y, sums, carry, scaled = local_scan(
        mixer_input,
        before,
        delta_raw,
        decay_rate,
        conv_weight,
        conv_bias.reshape(1, -1),
        skip_gain.reshape(SUB, LANES),
        in_flat,
        out_flat,
    )
    start = entering_state(carry, scaled)
    mixed = finish_scan(y, sums, start, scaled, gate_input, out_flat)
    rows = residual.shape[0]
    model_width = residual.shape[1]
    full_weight = lax.all_gather(out_weight, "seq", axis=1, tiled=True)
    projected = lax.psum_scatter(
        jnp.dot(mixed, full_weight, preferred_element_type=jnp.float32).astype(jnp.bfloat16),
        "exp",
        scatter_dimension=0,
        tiled=True,
    ).astype(jnp.float32)
    hidden_state = residual.astype(jnp.float32) + projected
    scale = lax.rsqrt(jnp.mean(hidden_state * hidden_state, axis=1, keepdims=True) + 1e-06)
    normed = (hidden_state * scale * norm_gain[None, :]).astype(jnp.bfloat16)
    experts = router_weight.shape[1]
    capacity = 2 * rows // experts + 1
    logits = jnp.dot(normed, router_weight, preferred_element_type=jnp.float32)
    expert_range = jnp.arange(experts, dtype=jnp.int32)
    matches = expert_ids[:, :, None] == expert_range[None, None, :]
    chosen = jnp.sum(jnp.where(matches, logits[:, None, :], 0.0), axis=2)
    first = jax.nn.sigmoid(chosen[:, 0] - chosen[:, 1])
    flat_ids = expert_ids.reshape(-1)
    position = jnp.arange(flat_ids.shape[0], dtype=jnp.int32)
    earlier = (flat_ids[:, None] == flat_ids[None, :]) & (position[None, :] < position[:, None])
    rank = jnp.sum(earlier.astype(jnp.int32), axis=1)
    target = flat_ids * capacity + rank
    placing = (jnp.arange(experts * capacity, dtype=jnp.int32)[:, None] == target[None, :]).astype(
        jnp.bfloat16
    )
    repeated = jnp.broadcast_to(normed[:, None, :], (rows, 2, model_width)).reshape(-1, model_width)
    outgoing = (
        jnp.dot(placing, repeated, preferred_element_type=jnp.float32)
        .astype(jnp.bfloat16)
        .reshape(experts, capacity, model_width)
    )
    arrived = lax.all_to_all(outgoing, "exp", split_axis=0, concat_axis=0, tiled=True)
    flat_rows = arrived.reshape(-1, arrived.shape[2])
    summed_out = experts_of_rows(flat_rows, gate_weight[0], up_weight[0], down_weight[0])
    returned = lax.all_to_all(
        summed_out.reshape(arrived.shape), "exp", split_axis=0, concat_axis=0, tiled=True
    )
    flat_returned = returned.reshape(-1, model_width)
    picked = jnp.einsum(
        "sa,sd->ad", placing, flat_returned, preferred_element_type=jnp.float32
    ).reshape(rows, 2, model_width)
    moe_out = first[:, None] * picked[:, 0] + (1.0 - first)[:, None] * picked[:, 1]
    final = (hidden_state + moe_out).astype(jnp.bfloat16)
    return (mixed, final)


def solution(mesh):
    return jax.shard_map(
        shards,
        mesh=mesh,
        in_specs=(
            P("seq", "exp"),
            P("seq", "exp"),
            P("seq", "exp"),
            P("seq", None),
            P("seq", None),
            P(None, "exp"),
            P(None, "exp"),
            P("exp"),
            P("exp"),
            P("exp", "seq"),
            P(("seq", "exp"), None),
            P(),
            P(),
            P(("seq", "exp"), None),
            P("exp", None, "seq"),
            P("exp", None, "seq"),
            P("exp", "seq", None),
        ),
        out_specs=(P("seq", "exp"), P(("seq", "exp"), None)),
        check_vma=False,
    )
```

```python
import functools
import math

import jax
import jax.numpy as jnp
from jax import lax
from jax.experimental import pallas as pl
from jax.experimental.pallas import tpu as pltpu
from jax.sharding import PartitionSpec as P

KCONV = 4
LANES = 128
SUB = 8
CORES = 2
SIDE = 4
LOG2E = math.log2(math.e)
VMEM = pl.BlockSpec(memory_space=pltpu.VMEM)
SMEM = pl.BlockSpec(memory_space=pltpu.SMEM)


def split_place(place):
    return place // (SIDE * CORES), (place // CORES) % SIDE, place % CORES


def join_place(y, x, c):
    return (y % SIDE * SIDE + x % SIDE) * CORES + c % CORES


def moved(block, dy=0, dx=0, dc=0):
    route = []
    for i in range(SIDE * SIDE * CORES):
        y, x, c = split_place(i)
        route.append((i, join_place(y + dy, x + dx, c + dc)))
    return lax.ppermute(block, "seq", route)


def local_scan_kernel(
    inp_ref, before_ref, raw_ref, rate_ref, taps_ref, bias_ref, skip_ref, in_ref, out_ref,
    y_ref, sums_ref, carry_ref, scaled_ref,
    pad_ref, delta_ref, conv_ref,
):
    length, width = inp_ref.shape
    states = rate_ref.shape[0]
    tiles = width // LANES
    for j in range(tiles):
        cols = slice(j * LANES, (j + 1) * LANES)
        pad_ref[SUB - KCONV + 1 : SUB, :] = before_ref[:, cols].astype(jnp.float32)
        pad_ref[SUB:, :] = inp_ref[:, cols].astype(jnp.float32)
        summed = jnp.broadcast_to(bias_ref[:, cols], (length, LANES))
        for k in range(KCONV):
            begin = SUB - KCONV + 1 + k
            summed = summed + taps_ref[k : k + 1, cols] * pad_ref[begin : begin + length, :]
        conv_ref[pl.ds(j, length, stride=tiles), :] = summed * jax.nn.sigmoid(summed)
        raw = raw_ref[:, cols].astype(jnp.float32)
        delta_ref[pl.ds(j, length, stride=tiles), :] = jnp.maximum(raw, 0.0) + jnp.log1p(
            jnp.exp(-jnp.abs(raw))
        )
        scaled_ref[pl.ds(j, states, stride=tiles), :] = rate_ref[:, cols] * -LOG2E

    skip = skip_ref[...]

    def step(t, carry):
        total, state = carry
        rows = pl.ds(pl.multiple_of(t * SUB, SUB), SUB)
        delta, value = delta_ref[rows, :], conv_ref[rows, :]
        total = total + delta
        out = skip * value
        after = []
        for n in range(states):
            retain = jnp.exp2(delta * scaled_ref[n * SUB : (n + 1) * SUB, :])
            fresh = in_ref[t * states + n] * value
            now = fresh + retain * (state[n] - fresh)
            out = out + out_ref[t * states + n] * now
            after.append(now)
        sums_ref[rows, :] = total
        y_ref[rows, :] = out
        return total, tuple(after)

    zero = jnp.zeros((SUB, LANES), jnp.float32)
    total, state = lax.fori_loop(0, length, step, (zero, (zero,) * states), unroll=2)
    for n in range(states):
        carry_ref[n * SUB : (n + 1) * SUB, :] = state[n]
    carry_ref[states * SUB :, :] = total


def finish_scan_kernel(y_ref, sums_ref, start_ref, scaled_ref, gate_ref, out_ref, mixed_ref, full_ref):
    length, width = gate_ref.shape
    states = start_ref.shape[0] // SUB
    tiles = width // LANES

    def step(t, carry):
        rows = pl.ds(pl.multiple_of(t * SUB, SUB), SUB)
        total, out = sums_ref[rows, :], y_ref[rows, :]
        for n in range(states):
            part = slice(n * SUB, (n + 1) * SUB)
            kept = jnp.exp2(total * scaled_ref[part, :]) * start_ref[part, :]
            out = out + out_ref[t * states + n] * kept
        full_ref[rows, :] = out
        return carry

    lax.fori_loop(0, length, step, 0, unroll=2)
    for j in range(tiles):
        cols = slice(j * LANES, (j + 1) * LANES)
        gate = gate_ref[:, cols].astype(jnp.float32)
        gated = full_ref[pl.ds(j, length, stride=tiles), :] * (gate * jax.nn.sigmoid(gate))
        mixed_ref[:, cols] = gated.astype(mixed_ref.dtype)


def local_scan(inp, before, raw, rate, taps, bias, skip, in_flat, out_flat):
    length, width = inp.shape
    states = rate.shape[0]
    flat = jax.ShapeDtypeStruct((length * SUB, LANES), jnp.float32)
    return pl.pallas_call(
        local_scan_kernel,
        name="local_scan",
        out_shape=(
            flat,
            flat,
            jax.ShapeDtypeStruct(((states + 1) * SUB, LANES), jnp.float32),
            jax.ShapeDtypeStruct((states * SUB, LANES), jnp.float32),
        ),
        in_specs=[VMEM] * 7 + [SMEM] * 2,
        out_specs=(VMEM,) * 4,
        scratch_shapes=[
            pltpu.VMEM((length + SUB, LANES), jnp.float32),
            pltpu.VMEM((length * SUB, LANES), jnp.float32),
            pltpu.VMEM((length * SUB, LANES), jnp.float32),
        ],
        compiler_params=pltpu.CompilerParams(vmem_limit_bytes=24 << 20),
        cost_estimate=pl.CostEstimate(flops=8_000_000, transcendentals=2_500_000, bytes_accessed=2_000_000),
    )(inp, before, raw, rate, taps, bias, skip, in_flat, out_flat)


def finish_scan(y, sums, start, scaled, gate, out_flat):
    length, width = gate.shape
    return pl.pallas_call(
        finish_scan_kernel,
        name="finish_scan",
        out_shape=jax.ShapeDtypeStruct((length, width), jnp.bfloat16),
        in_specs=[VMEM] * 5 + [SMEM],
        out_specs=VMEM,
        scratch_shapes=[pltpu.VMEM((length * SUB, LANES), jnp.float32)],
        compiler_params=pltpu.CompilerParams(vmem_limit_bytes=24 << 20),
        cost_estimate=pl.CostEstimate(flops=8_000_000, transcendentals=2_500_000, bytes_accessed=2_000_000),
    )(y, sums, start, scaled, gate, out_flat)


def entering_state(carry, scaled):
    states = scaled.shape[0] // SUB
    scaled = scaled.reshape(states, SUB, LANES)
    y, x, c = split_place(lax.axis_index("seq"))

    def parts(block):
        block = block.reshape(states + 1, SUB, LANES)
        return block[states], block[:states]

    def kept(span, state):
        return jnp.exp2(span[None] * scaled) * state

    def packed(span, state):
        return jnp.concatenate([state, span[None]], axis=0).reshape(carry.shape)

    own = parts(carry)
    other = parts(moved(carry, dc=1))
    is_first = c == 0
    first = [jnp.where(is_first, a, b) for a, b in zip(own, other)]
    last = [jnp.where(is_first, b, a) for a, b in zip(own, other)]
    chip = (first[0] + last[0], kept(last[0], first[1]) + last[1])
    start = jnp.where(is_first, 0.0, other[1])
    span = jnp.where(is_first, 0.0, other[0])

    sent = packed(*chip)
    near = [parts(moved(sent, dx=k)) for k in range(1, SIDE)]
    ahead = jnp.zeros_like(span)
    behind = jnp.zeros_like(span)
    row_state = jnp.zeros_like(chip[1])
    earlier_state = jnp.zeros_like(chip[1])
    for k in range(1, SIDE):
        got_span, got_state = near[k - 1]
        is_earlier = k <= x
        earlier_state = earlier_state + jnp.where(is_earlier, kept(ahead, got_state), 0.0)
        row_state = row_state + jnp.where(is_earlier, 0.0, kept(behind, got_state))
        ahead = ahead + jnp.where(is_earlier, got_span, 0.0)
        behind = behind + jnp.where(is_earlier, 0.0, got_span)
    row_state = row_state + kept(behind, chip[1] + kept(chip[0], earlier_state))
    row_span = ahead + chip[0] + behind
    start = start + kept(span, earlier_state)
    span = span + ahead

    sent = packed(row_span, row_state)
    far = [parts(moved(sent, dy=k)) for k in range(1, SIDE)]
    for k in range(1, SIDE):
        got_span, got_state = far[k - 1]
        is_earlier = k <= y
        start = start + jnp.where(is_earlier, kept(span, got_state), 0.0)
        span = span + jnp.where(is_earlier, got_span, 0.0)
    return start.reshape(states * SUB, LANES)


def from_before(tail):
    count = lax.axis_size("seq")
    return lax.ppermute(tail, "seq", [(i, i + 1) for i in range(count - 1)])


def around(block, along, step):
    return moved(block, dy=step) if along == "y" else moved(block, dx=step)


def gather_rows(block, inner, outer):
    near = [block] + [around(block, inner, k) for k in range(1, SIDE)]
    low, high = jnp.concatenate(near[:2], axis=0), jnp.concatenate(near[2:], axis=0)
    low_up = around(low, outer, 1)
    high_down = around(high, outer, -1)
    high_up = around(high, outer, 1)
    low_down = around(low, outer, -1)
    low_far = around(low_up, outer, 1)
    high_far = around(high_down, outer, -1)
    return (low, high), (low_up, high_up), (low_far, high_far), (low_down, high_down)


def added(*terms):
    return sum(t.astype(jnp.float32) for t in terms)


def scatter_sums(groups, inner, outer):
    (low, high), (low_up, high_up), (low_far, high_far), (low_down, high_down) = groups
    dtype = low.dtype
    low_relay = around(low_far, outer, 1)
    high_relay = around(high_far, outer, -1)
    got_high_down = around(high_down, outer, 1)
    got_low_up = around(low_up, outer, -1)
    got_low_down = around(added(low_down, low_relay).astype(dtype), outer, 1)
    got_high_up = around(added(high_up, high_relay).astype(dtype), outer, -1)
    low_sum = added(low, got_low_down, got_low_up)
    high_sum = added(high, got_high_down, got_high_up)
    rows = low.shape[0] // 2
    blocks = [low_sum[:rows], low_sum[rows:], high_sum[:rows], high_sum[rows:]]
    near = [around(blocks[k].astype(dtype), inner, -k) for k in range(1, SIDE)]
    return added(blocks[0], *near).astype(dtype)


def expert_in_kernel(*refs):
    pieces, (gate_a, gate_b, up_a, up_b, act_a, act_b, rows_ref) = refs[:16], refs[16:]
    half, width = pieces[0].shape
    rows = half // 2

    @pl.when(pl.program_id(0) == 0)
    def _():
        for k in range(SIDE):
            for h in range(2):
                begin = (2 * k + h) * half
                rows_ref[begin : begin + half, :width] = pieces[2 * k + h][...]
                for i in range(2):
                    begin = ((2 * h + i) * SIDE + k) * rows
                    block = pieces[8 + 2 * k + h][i * rows : (i + 1) * rows, :]
                    rows_ref[begin : begin + rows, width:] = block

    for gate, up, act in ((gate_a, up_a, act_a), (gate_b, up_b, act_b)):
        both = jnp.concatenate([gate[...], up[...]], axis=1)
        hidden = jnp.dot(rows_ref[...], both, preferred_element_type=jnp.float32)
        gating, upward = hidden[:, :LANES], hidden[:, LANES:]
        act[...] = (gating * jax.nn.sigmoid(gating) * upward).astype(act.dtype)


def expert_in(pieces, gate_a, gate_b, up_a, up_b):
    half, width = pieces[0].shape
    count = 2 * SIDE * half
    hidden = gate_a.shape[1]
    weight = pl.BlockSpec((2 * width, LANES), lambda i: (0, i))
    act = pl.BlockSpec((count, LANES), lambda i: (0, i))
    out = jax.ShapeDtypeStruct((count, hidden), jnp.bfloat16)
    return pl.pallas_call(
        expert_in_kernel,
        name="expert_in",
        grid=(hidden // LANES,),
        out_shape=(out, out),
        in_specs=[VMEM] * 16 + [weight] * 4,
        out_specs=(act, act),
        scratch_shapes=[pltpu.VMEM((count, 2 * width), jnp.bfloat16)],
        compiler_params=pltpu.CompilerParams(vmem_limit_bytes=48 << 20),
        cost_estimate=pl.CostEstimate(
            flops=8 * count * width * hidden * 2, transcendentals=2 * count * hidden, bytes_accessed=20_000_000
        ),
    )(*pieces, gate_a, gate_b, up_a, up_b)


def expert_out_kernel(by_outer, act_a, act_b, down_a, down_b, *outs):
    half = outs[0].shape[0]
    rows = half // 2
    acts = jnp.concatenate([act_a[...], act_b[...]], axis=1)
    down = jnp.concatenate([down_a[...], down_b[...]], axis=0)
    result = jnp.dot(acts, down, preferred_element_type=jnp.float32).astype(outs[0].dtype)
    for k in range(SIDE):
        for h in range(2):
            if by_outer:
                begin = (2 * k + h) * half
                outs[2 * k + h][...] = result[begin : begin + half]
            else:
                for i in range(2):
                    begin = ((2 * h + i) * SIDE + k) * rows
                    outs[2 * k + h][i * rows : (i + 1) * rows, :] = result[begin : begin + rows]


def expert_out(by_outer, act_a, act_b, down_a, down_b):
    count, hidden = act_a.shape
    width = down_a.shape[1] // 2
    tile = 4 * LANES
    tiles = width // tile
    skip = 0 if by_outer else tiles
    half = count // (2 * SIDE)
    weight = pl.BlockSpec((hidden, tile), lambda i: (0, i + skip))
    piece = pl.BlockSpec((half, tile), lambda i: (0, i))
    out = jax.ShapeDtypeStruct((half, width), jnp.bfloat16)
    outs = pl.pallas_call(
        functools.partial(expert_out_kernel, by_outer),
        name="expert_out",
        grid=(tiles,),
        out_shape=(out,) * 8,
        in_specs=[VMEM] * 2 + [weight] * 2,
        out_specs=(piece,) * 8,
        compiler_params=pltpu.CompilerParams(vmem_limit_bytes=32 << 20),
        cost_estimate=pl.CostEstimate(
            flops=4 * count * width * hidden, transcendentals=0, bytes_accessed=8_000_000
        ),
    )(act_a, act_b, down_a, down_b)
    return [outs[2 * k : 2 * k + 2] for k in range(SIDE)]


def experts_of_rows(rows, gate, up, down, other_gate, other_up, other_down):
    width = rows.shape[1] // 2
    first = gather_rows(rows[:, :width], "x", "y")
    second = gather_rows(rows[:, width:], "y", "x")
    pieces = [p for groups in (first, second) for pair in groups for p in pair]
    act, other_act = expert_in(pieces, gate, other_gate, up, other_up)
    first = expert_out(True, act, other_act, down, other_down)
    second = expert_out(False, act, other_act, down, other_down)
    return jnp.concatenate(
        [scatter_sums(first, "x", "y"), scatter_sums(second, "y", "x")], axis=1
    )


def along_experts(block, step):
    count = lax.axis_size("exp")
    return lax.ppermute(block, "exp", [(i, (i + step) % count) for i in range(count)])


def project_kernel(me_ref, own_ref, other_ref, weight_ref, out_ref):
    owners, rows = out_ref.shape[0], out_ref.shape[1] // CORES
    tokens = own_ref.shape[0]
    both = jnp.concatenate([weight_ref[0], weight_ref[1]], axis=1)
    mixed = jnp.concatenate([own_ref[...], other_ref[...]], axis=0)
    result = jnp.dot(mixed, both, preferred_element_type=jnp.float32).astype(out_ref.dtype)
    for owner in range(owners):
        place = lax.rem(owner - me_ref[0] + owners, owners)
        for core in range(CORES):
            begin = core * tokens + owner * rows
            out_ref[place, core * rows : (core + 1) * rows, :] = result[begin : begin + rows]


def project(mixed, weight):
    chips = SIDE * SIDE
    groups = [[j * CORES + c for j in range(chips)] for c in range(CORES)]
    spread = jnp.broadcast_to(weight[None], (chips,) + weight.shape)
    columns = lax.all_to_all(spread, "seq", 0, 0, axis_index_groups=groups, tiled=True)
    other = moved(mixed, dc=1)
    owners = lax.axis_size("exp")
    tokens, depth = mixed.shape
    rows = tokens // owners
    terms = pl.pallas_call(
        project_kernel,
        name="project",
        grid=(chips // 2,),
        out_shape=jax.ShapeDtypeStruct((owners, CORES * rows, chips * LANES), jnp.bfloat16),
        in_specs=[SMEM, VMEM, VMEM, pl.BlockSpec((2, depth, LANES), lambda i: (i, 0, 0))],
        out_specs=pl.BlockSpec((owners, CORES * rows, 2 * LANES), lambda i: (0, 0, i)),
        compiler_params=pltpu.CompilerParams(vmem_limit_bytes=24 << 20),
        cost_estimate=pl.CostEstimate(
            flops=2 * CORES * tokens * depth * chips * LANES, transcendentals=0, bytes_accessed=6_000_000
        ),
    )(lax.axis_index("exp").reshape(1), mixed, other, columns)
    total = added(terms[0], *(along_experts(terms[k], k) for k in range(1, owners)))
    mine = total[:rows]
    traded = moved(total[rows:], dc=1)
    is_first = lax.axis_index("seq") % CORES == 0
    halves = [jnp.where(is_first, a, b).reshape(rows, chips, LANES) for a, b in ((mine, traded), (traded, mine))]
    return jnp.stack(halves, axis=2).reshape(rows, -1)


def shards(
    mixer_input,
    gate_input,
    delta_raw,
    input_coef,
    output_coef,
    decay_rate,
    conv_weight,
    conv_bias,
    skip_gain,
    out_weight,
    residual,
    norm_gain,
    router_weight,
    expert_ids,
    gate_weight,
    up_weight,
    down_weight,
):
    length = mixer_input.shape[0]
    in_flat = input_coef.astype(jnp.float32).reshape(-1)
    out_flat = output_coef.astype(jnp.float32).reshape(-1)
    before = from_before(mixer_input[length - (KCONV - 1) :])
    y, sums, carry, scaled = local_scan(
        mixer_input,
        before,
        delta_raw,
        decay_rate,
        conv_weight,
        conv_bias.reshape(1, -1),
        skip_gain.reshape(SUB, LANES),
        in_flat,
        out_flat,
    )
    experts_here = [w[0] for w in (gate_weight, up_weight, down_weight)]
    experts_there = [moved(w, dc=1) for w in experts_here]
    carry, *experts_there = lax.optimization_barrier((carry, *experts_there))
    start = entering_state(carry, scaled)
    mixed = finish_scan(y, sums, start, scaled, gate_input, out_flat)
    rows = residual.shape[0]
    model_width = residual.shape[1]
    projected = project(mixed, out_weight)
    hidden_state = residual.astype(jnp.float32) + projected
    scale = lax.rsqrt(jnp.mean(hidden_state * hidden_state, axis=1, keepdims=True) + 1e-06)
    normed = (hidden_state * scale * norm_gain[None, :]).astype(jnp.bfloat16)
    experts = router_weight.shape[1]
    capacity = 2 * rows // experts + 1
    logits = jnp.dot(normed, router_weight, preferred_element_type=jnp.float32)
    expert_range = jnp.arange(experts, dtype=jnp.int32)
    matches = expert_ids[:, :, None] == expert_range[None, None, :]
    chosen = jnp.sum(jnp.where(matches, logits[:, None, :], 0.0), axis=2)
    first = jax.nn.sigmoid(chosen[:, 0] - chosen[:, 1])
    flat_ids = expert_ids.reshape(-1)
    position = jnp.arange(flat_ids.shape[0], dtype=jnp.int32)
    earlier = (flat_ids[:, None] == flat_ids[None, :]) & (position[None, :] < position[:, None])
    rank = jnp.sum(earlier.astype(jnp.int32), axis=1)
    turn = (flat_ids - lax.axis_index("exp") + experts) % experts
    target = turn * capacity + rank
    placing = (jnp.arange(experts * capacity, dtype=jnp.int32)[:, None] == target[None, :]).astype(
        jnp.bfloat16
    )
    repeated = jnp.broadcast_to(normed[:, None, :], (rows, 2, model_width)).reshape(-1, model_width)
    outgoing = jnp.dot(placing, repeated, preferred_element_type=jnp.float32).astype(jnp.bfloat16)
    outgoing = outgoing.reshape(experts, -1, LANES)
    arrived = [outgoing[0]] + [along_experts(outgoing[k], k) for k in range(1, experts)]
    flat_rows = jnp.concatenate(arrived, axis=0).reshape(-1, model_width)
    summed_out = experts_of_rows(flat_rows, *experts_here, *experts_there)
    summed_out = summed_out.reshape(experts, -1, LANES)
    returned = [summed_out[0]] + [along_experts(summed_out[k], -k) for k in range(1, experts)]
    flat_returned = jnp.concatenate(returned, axis=0).reshape(-1, model_width)
    picked = jnp.einsum(
        "sa,sd->ad", placing, flat_returned, preferred_element_type=jnp.float32
    ).reshape(rows, 2, model_width)
    moe_out = first[:, None] * picked[:, 0] + (1.0 - first)[:, None] * picked[:, 1]
    final = (hidden_state + moe_out).astype(jnp.bfloat16)
    return (mixed, final)


def solution(mesh):
    return jax.shard_map(
        shards,
        mesh=mesh,
        in_specs=(
            P("seq", "exp"),
            P("seq", "exp"),
            P("seq", "exp"),
            P("seq", None),
            P("seq", None),
            P(None, "exp"),
            P(None, "exp"),
            P("exp"),
            P("exp"),
            P("exp", "seq"),
            P(("seq", "exp"), None),
            P(),
            P(),
            P(("seq", "exp"), None),
            P("exp", None, "seq"),
            P("exp", None, "seq"),
            P("exp", "seq", None),
        ),
        out_specs=(P("seq", "exp"), P(("seq", "exp"), None)),
        check_vma=False,
    )
```

```python
import functools
import math

import jax
import jax.numpy as jnp
from jax import lax
from jax.experimental import pallas as pl
from jax.experimental.pallas import tpu as pltpu
from jax.sharding import PartitionSpec as P

KCONV = 4
LANES = 128
SUB = 8
CORES = 2
SIDE = 4
LOG2E = math.log2(math.e)
VMEM = pl.BlockSpec(memory_space=pltpu.VMEM)
SMEM = pl.BlockSpec(memory_space=pltpu.SMEM)


def split_place(place):
    return place // (SIDE * CORES), (place // CORES) % SIDE, place % CORES


def join_place(y, x, c):
    return (y % SIDE * SIDE + x % SIDE) * CORES + c % CORES


def moved(block, dy=0, dx=0, dc=0):
    route = []
    for i in range(SIDE * SIDE * CORES):
        y, x, c = split_place(i)
        route.append((i, join_place(y + dy, x + dx, c + dc)))
    return lax.ppermute(block, "seq", route)


def local_scan_kernel(
    inp_ref, before_ref, raw_ref, rate_ref, taps_ref, bias_ref, skip_ref, in_ref, out_ref,
    y_ref, sums_ref, carry_ref, scaled_ref,
    pad_ref, delta_ref, conv_ref,
):
    length, width = inp_ref.shape
    states = rate_ref.shape[0]
    tiles = width // LANES
    for j in range(tiles):
        cols = slice(j * LANES, (j + 1) * LANES)
        pad_ref[SUB - KCONV + 1 : SUB, :] = before_ref[:, cols].astype(jnp.float32)
        pad_ref[SUB:, :] = inp_ref[:, cols].astype(jnp.float32)
        summed = jnp.broadcast_to(bias_ref[:, cols], (length, LANES))
        for k in range(KCONV):
            begin = SUB - KCONV + 1 + k
            summed = summed + taps_ref[k : k + 1, cols] * pad_ref[begin : begin + length, :]
        conv_ref[pl.ds(j, length, stride=tiles), :] = summed * jax.nn.sigmoid(summed)
        raw = raw_ref[:, cols].astype(jnp.float32)
        delta_ref[pl.ds(j, length, stride=tiles), :] = jnp.maximum(raw, 0.0) + jnp.log1p(
            jnp.exp(-jnp.abs(raw))
        )
        scaled_ref[pl.ds(j, states, stride=tiles), :] = rate_ref[:, cols] * -LOG2E

    skip = skip_ref[...]

    def step(t, carry):
        total, state = carry
        rows = pl.ds(pl.multiple_of(t * SUB, SUB), SUB)
        delta, value = delta_ref[rows, :], conv_ref[rows, :]
        total = total + delta
        out = skip * value
        after = []
        for n in range(states):
            retain = jnp.exp2(delta * scaled_ref[n * SUB : (n + 1) * SUB, :])
            fresh = in_ref[t * states + n] * value
            now = fresh + retain * (state[n] - fresh)
            out = out + out_ref[t * states + n] * now
            after.append(now)
        sums_ref[rows, :] = total
        y_ref[rows, :] = out
        return total, tuple(after)

    zero = jnp.zeros((SUB, LANES), jnp.float32)
    total, state = lax.fori_loop(0, length, step, (zero, (zero,) * states), unroll=2)
    for n in range(states):
        carry_ref[n * SUB : (n + 1) * SUB, :] = state[n]
    carry_ref[states * SUB :, :] = total


def finish_scan_kernel(y_ref, sums_ref, start_ref, scaled_ref, gate_ref, out_ref, mixed_ref, full_ref):
    length, width = gate_ref.shape
    states = start_ref.shape[0] // SUB
    tiles = width // LANES

    def step(t, carry):
        rows = pl.ds(pl.multiple_of(t * SUB, SUB), SUB)
        total, out = sums_ref[rows, :], y_ref[rows, :]
        for n in range(states):
            part = slice(n * SUB, (n + 1) * SUB)
            kept = jnp.exp2(total * scaled_ref[part, :]) * start_ref[part, :]
            out = out + out_ref[t * states + n] * kept
        full_ref[rows, :] = out
        return carry

    lax.fori_loop(0, length, step, 0, unroll=2)
    for j in range(tiles):
        cols = slice(j * LANES, (j + 1) * LANES)
        gate = gate_ref[:, cols].astype(jnp.float32)
        gated = full_ref[pl.ds(j, length, stride=tiles), :] * (gate * jax.nn.sigmoid(gate))
        mixed_ref[:, cols] = gated.astype(mixed_ref.dtype)


def local_scan(inp, before, raw, rate, taps, bias, skip, in_flat, out_flat):
    length, width = inp.shape
    states = rate.shape[0]
    flat = jax.ShapeDtypeStruct((length * SUB, LANES), jnp.float32)
    return pl.pallas_call(
        local_scan_kernel,
        name="local_scan",
        out_shape=(
            flat,
            flat,
            jax.ShapeDtypeStruct(((states + 1) * SUB, LANES), jnp.float32),
            jax.ShapeDtypeStruct((states * SUB, LANES), jnp.float32),
        ),
        in_specs=[VMEM] * 7 + [SMEM] * 2,
        out_specs=(VMEM,) * 4,
        scratch_shapes=[
            pltpu.VMEM((length + SUB, LANES), jnp.float32),
            pltpu.VMEM((length * SUB, LANES), jnp.float32),
            pltpu.VMEM((length * SUB, LANES), jnp.float32),
        ],
        compiler_params=pltpu.CompilerParams(vmem_limit_bytes=24 << 20),
        cost_estimate=pl.CostEstimate(flops=8_000_000, transcendentals=2_500_000, bytes_accessed=2_000_000),
    )(inp, before, raw, rate, taps, bias, skip, in_flat, out_flat)


def finish_scan(y, sums, start, scaled, gate, out_flat):
    length, width = gate.shape
    return pl.pallas_call(
        finish_scan_kernel,
        name="finish_scan",
        out_shape=jax.ShapeDtypeStruct((length, width), jnp.bfloat16),
        in_specs=[VMEM] * 5 + [SMEM],
        out_specs=VMEM,
        scratch_shapes=[pltpu.VMEM((length * SUB, LANES), jnp.float32)],
        compiler_params=pltpu.CompilerParams(vmem_limit_bytes=24 << 20),
        cost_estimate=pl.CostEstimate(flops=8_000_000, transcendentals=2_500_000, bytes_accessed=2_000_000),
    )(y, sums, start, scaled, gate, out_flat)


def entering_state(carry, scaled):
    states = scaled.shape[0] // SUB
    scaled = scaled.reshape(states, SUB, LANES)
    y, x, c = split_place(lax.axis_index("seq"))

    def parts(block):
        block = block.reshape(states + 1, SUB, LANES)
        return block[states], block[:states]

    def kept(span, state):
        return jnp.exp2(span[None] * scaled) * state

    def packed(span, state):
        return jnp.concatenate([state, span[None]], axis=0).reshape(carry.shape)

    own = parts(carry)
    other = parts(moved(carry, dc=1))
    is_first = c == 0
    first = [jnp.where(is_first, a, b) for a, b in zip(own, other)]
    last = [jnp.where(is_first, b, a) for a, b in zip(own, other)]
    chip = (first[0] + last[0], kept(last[0], first[1]) + last[1])
    start = jnp.where(is_first, 0.0, other[1])
    span = jnp.where(is_first, 0.0, other[0])

    sent = packed(*chip)
    near = [parts(moved(sent, dx=k)) for k in range(1, SIDE)]
    ahead = jnp.zeros_like(span)
    behind = jnp.zeros_like(span)
    row_state = jnp.zeros_like(chip[1])
    earlier_state = jnp.zeros_like(chip[1])
    for k in range(1, SIDE):
        got_span, got_state = near[k - 1]
        is_earlier = k <= x
        earlier_state = earlier_state + jnp.where(is_earlier, kept(ahead, got_state), 0.0)
        row_state = row_state + jnp.where(is_earlier, 0.0, kept(behind, got_state))
        ahead = ahead + jnp.where(is_earlier, got_span, 0.0)
        behind = behind + jnp.where(is_earlier, 0.0, got_span)
    row_state = row_state + kept(behind, chip[1] + kept(chip[0], earlier_state))
    row_span = ahead + chip[0] + behind
    start = start + kept(span, earlier_state)
    span = span + ahead

    sent = packed(row_span, row_state)
    far = [parts(moved(sent, dy=k)) for k in range(1, SIDE)]
    for k in range(1, SIDE):
        got_span, got_state = far[k - 1]
        is_earlier = k <= y
        start = start + jnp.where(is_earlier, kept(span, got_state), 0.0)
        span = span + jnp.where(is_earlier, got_span, 0.0)
    return start.reshape(states * SUB, LANES)


def from_before(tail):
    count = lax.axis_size("seq")
    return lax.ppermute(tail, "seq", [(i, i + 1) for i in range(count - 1)])


def around(block, ring, step):
    route = []
    for i in range(SIDE * SIDE * CORES):
        y, x, c = split_place(i)
        along_x = (ring == "inner") == (c == 0)
        dy, dx = (0, step) if along_x else (step, 0)
        route.append((i, join_place(y + dy, x + dx, c)))
    return lax.ppermute(block, "seq", route)


def added(*terms):
    return sum(t.astype(jnp.float32) for t in terms)


def expert_in_kernel(*refs):
    pieces, (gate_a, gate_b, up_a, up_b, act_a, act_b, rows_ref) = refs[:-7], refs[-7:]
    rows = pieces[0].shape[0]

    @pl.when(pl.program_id(0) == 0)
    def _():
        for k, piece in enumerate(pieces):
            rows_ref[k * rows : (k + 1) * rows, :] = piece[...]

    for gate, up, act in ((gate_a, up_a, act_a), (gate_b, up_b, act_b)):
        both = jnp.concatenate([gate[...], up[...]], axis=1)
        hidden = jnp.dot(rows_ref[...], both, preferred_element_type=jnp.float32)
        gating, upward = hidden[:, :LANES], hidden[:, LANES:]
        act[...] = (gating * jax.nn.sigmoid(gating) * upward).astype(act.dtype)


def expert_out_kernel(act_a, act_b, down_a, down_b, *outs):
    rows = outs[0].shape[0]
    acts = jnp.concatenate([act_a[...], act_b[...]], axis=1)
    down = jnp.concatenate([down_a[...], down_b[...]], axis=0)
    result = jnp.dot(acts, down, preferred_element_type=jnp.float32).astype(outs[0].dtype)
    for k, out in enumerate(outs):
        out[...] = result[k * rows : (k + 1) * rows]


def expert(pieces, here, there):
    rows, width = pieces[0].shape
    count = len(pieces) * rows
    hidden = here[0].shape[1]
    weight = pl.BlockSpec((width, LANES), lambda i: (0, i))
    act = pl.BlockSpec((count, LANES), lambda i: (0, i))
    acts = pl.pallas_call(
        expert_in_kernel,
        name="expert_in",
        grid=(hidden // LANES,),
        out_shape=(jax.ShapeDtypeStruct((count, hidden), jnp.bfloat16),) * 2,
        in_specs=[VMEM] * len(pieces) + [weight] * 4,
        out_specs=(act, act),
        scratch_shapes=[pltpu.VMEM((count, width), jnp.bfloat16)],
        compiler_params=pltpu.CompilerParams(vmem_limit_bytes=32 << 20),
        cost_estimate=pl.CostEstimate(
            flops=8 * count * width * hidden, transcendentals=2 * count * hidden, bytes_accessed=20_000_000
        ),
    )(*pieces, here[0], there[0], here[1], there[1])
    tile = 4 * LANES
    weight = pl.BlockSpec((hidden, tile), lambda i: (0, i))
    piece = pl.BlockSpec((rows, tile), lambda i: (0, i))
    return pl.pallas_call(
        expert_out_kernel,
        name="expert_out",
        grid=(width // tile,),
        out_shape=(jax.ShapeDtypeStruct((rows, width), jnp.bfloat16),) * len(pieces),
        in_specs=[VMEM] * 2 + [weight] * 2,
        out_specs=(piece,) * len(pieces),
        compiler_params=pltpu.CompilerParams(vmem_limit_bytes=32 << 20),
        cost_estimate=pl.CostEstimate(
            flops=4 * count * width * hidden, transcendentals=0, bytes_accessed=10_000_000
        ),
    )(*acts, here[2], there[2])


def experts_of_rows(block, here, there):
    dtype = block.dtype
    near = [block] + [around(block, "inner", k) for k in range(1, SIDE)]
    low, high = jnp.concatenate(near[:2], axis=0), jnp.concatenate(near[2:], axis=0)
    low_up = around(low, "outer", 1)
    high_down = around(high, "outer", -1)
    high_up = around(high, "outer", 1)
    low_down = around(low, "outer", -1)
    low_far = around(low_up, "outer", 1)
    high_far = around(high_down, "outer", -1)
    low, high, low_up, high_down = expert([low, high, low_up, high_down], here, there)
    got_high_down = around(high_down, "outer", 1)
    got_low_up = around(low_up, "outer", -1)
    low_far, high_far, low_down, high_up = expert([low_far, high_far, low_down, high_up], here, there)
    low_relay = around(low_far, "outer", 1)
    high_relay = around(high_far, "outer", -1)
    got_low_down = around(added(low_down, low_relay).astype(dtype), "outer", 1)
    got_high_up = around(added(high_up, high_relay).astype(dtype), "outer", -1)
    low_sum = added(low, got_low_up, got_low_down)
    high_sum = added(high, got_high_down, got_high_up)
    rows = block.shape[0]
    blocks = [low_sum[:rows], low_sum[rows:], high_sum[:rows], high_sum[rows:]]
    back = [around(blocks[k].astype(dtype), "inner", -k) for k in range(1, SIDE)]
    return added(blocks[0], *back).astype(dtype)


def project_kernel(mixed_ref, weight_ref, out_ref):
    owners, rows = out_ref.shape[:2]
    both = jnp.concatenate([weight_ref[0], weight_ref[1]], axis=1)
    result = jnp.dot(mixed_ref[...], both, preferred_element_type=jnp.float32).astype(out_ref.dtype)
    for owner in range(owners):
        out_ref[owner] = result[owner * rows : (owner + 1) * rows]


def project(mixed, weight):
    blocks = lax.all_gather(weight, "seq")
    owners = lax.axis_size("exp")
    tokens, depth = mixed.shape
    count = blocks.shape[0]
    rows = tokens // owners
    terms = pl.pallas_call(
        project_kernel,
        name="project",
        grid=(count // 2,),
        out_shape=jax.ShapeDtypeStruct((owners, rows, count * LANES), jnp.bfloat16),
        in_specs=[VMEM, pl.BlockSpec((2, depth, LANES), lambda i: (i, 0, 0))],
        out_specs=pl.BlockSpec((owners, rows, 2 * LANES), lambda i: (0, 0, i)),
        compiler_params=pltpu.CompilerParams(vmem_limit_bytes=24 << 20),
        cost_estimate=pl.CostEstimate(
            flops=2 * tokens * depth * count * LANES, transcendentals=0, bytes_accessed=10_000_000
        ),
    )(mixed, blocks)
    terms = lax.all_to_all(terms, "exp", 0, 0, tiled=True)
    return added(*(terms[k] for k in range(owners)))


def shards(
    mixer_input,
    gate_input,
    delta_raw,
    input_coef,
    output_coef,
    decay_rate,
    conv_weight,
    conv_bias,
    skip_gain,
    out_weight,
    residual,
    norm_gain,
    router_weight,
    expert_ids,
    gate_weight,
    up_weight,
    down_weight,
):
    length = mixer_input.shape[0]
    in_flat = input_coef.astype(jnp.float32).reshape(-1)
    out_flat = output_coef.astype(jnp.float32).reshape(-1)
    before = from_before(mixer_input[length - (KCONV - 1) :])
    y, sums, carry, scaled = local_scan(
        mixer_input,
        before,
        delta_raw,
        decay_rate,
        conv_weight,
        conv_bias.reshape(1, -1),
        skip_gain.reshape(SUB, LANES),
        in_flat,
        out_flat,
    )
    here = [w[0] for w in (gate_weight, up_weight, down_weight)]
    there = [moved(w, dc=1) for w in here]
    carry, *there = lax.optimization_barrier((carry, *there))
    start = entering_state(carry, scaled)
    mixed = finish_scan(y, sums, start, scaled, gate_input, out_flat)
    rows = residual.shape[0]
    model_width = residual.shape[1]
    projected = project(mixed, out_weight)
    hidden_state = residual.astype(jnp.float32) + projected
    scale = lax.rsqrt(jnp.mean(hidden_state * hidden_state, axis=1, keepdims=True) + 1e-06)
    normed = (hidden_state * scale * norm_gain[None, :]).astype(jnp.bfloat16)
    experts = router_weight.shape[1]
    capacity = 2 * rows // experts + 1
    logits = jnp.dot(normed, router_weight, preferred_element_type=jnp.float32)
    expert_range = jnp.arange(experts, dtype=jnp.int32)
    matches = expert_ids[:, :, None] == expert_range[None, None, :]
    chosen = jnp.sum(jnp.where(matches, logits[:, None, :], 0.0), axis=2)
    first = jax.nn.sigmoid(chosen[:, 0] - chosen[:, 1])
    flat_ids = expert_ids.reshape(-1)
    position = jnp.arange(flat_ids.shape[0], dtype=jnp.int32)
    earlier = (flat_ids[:, None] == flat_ids[None, :]) & (position[None, :] < position[:, None])
    rank = jnp.sum(earlier.astype(jnp.int32), axis=1)
    target = flat_ids * capacity + rank
    placing = (jnp.arange(experts * capacity, dtype=jnp.int32)[:, None] == target[None, :]).astype(
        jnp.bfloat16
    )
    repeated = jnp.broadcast_to(normed[:, None, :], (rows, 2, model_width)).reshape(-1, model_width)
    outgoing = (
        jnp.dot(placing, repeated, preferred_element_type=jnp.float32)
        .astype(jnp.bfloat16)
        .reshape(experts, capacity, model_width)
    )
    arrived = lax.all_to_all(outgoing, "exp", split_axis=0, concat_axis=0, tiled=True)
    flat_rows = arrived.reshape(-1, arrived.shape[2])
    summed_out = experts_of_rows(flat_rows, here, there)
    returned = lax.all_to_all(
        summed_out.reshape(arrived.shape), "exp", split_axis=0, concat_axis=0, tiled=True
    )
    flat_returned = returned.reshape(-1, model_width)
    picked = jnp.einsum(
        "sa,sd->ad", placing, flat_returned, preferred_element_type=jnp.float32
    ).reshape(rows, 2, model_width)
    moe_out = first[:, None] * picked[:, 0] + (1.0 - first)[:, None] * picked[:, 1]
    final = (hidden_state + moe_out).astype(jnp.bfloat16)
    return (mixed, final)


def solution(mesh):
    return jax.shard_map(
        shards,
        mesh=mesh,
        in_specs=(
            P("seq", "exp"),
            P("seq", "exp"),
            P("seq", "exp"),
            P("seq", None),
            P("seq", None),
            P(None, "exp"),
            P(None, "exp"),
            P("exp"),
            P("exp"),
            P("exp", "seq"),
            P(("seq", "exp"), None),
            P(),
            P(),
            P(("seq", "exp"), None),
            P("exp", None, "seq"),
            P("exp", None, "seq"),
            P("exp", "seq", None),
        ),
        out_specs=(P("seq", "exp"), P(("seq", "exp"), None)),
        check_vma=False,
    )
```

```python
import functools
import math

import jax
import jax.numpy as jnp
from jax import lax
from jax.experimental import pallas as pl
from jax.experimental.pallas import tpu as pltpu
from jax.sharding import PartitionSpec as P

KCONV = 4
LANES = 128
SUB = 8
CORES = 2
SIDE = 4
LOG2E = math.log2(math.e)
VMEM = pl.BlockSpec(memory_space=pltpu.VMEM)
SMEM = pl.BlockSpec(memory_space=pltpu.SMEM)
HBM = pl.BlockSpec(memory_space=pltpu.MemorySpace.HBM)


def split_place(place):
    return place // (SIDE * CORES), (place // CORES) % SIDE, place % CORES


def join_place(y, x, c):
    return (y % SIDE * SIDE + x % SIDE) * CORES + c % CORES


def moved(block, dy=0, dx=0, dc=0):
    route = []
    for i in range(SIDE * SIDE * CORES):
        y, x, c = split_place(i)
        route.append((i, join_place(y + dy, x + dx, c + dc)))
    return lax.ppermute(block, "seq", route)


def local_scan_kernel(
    inp_hbm, raw_hbm, rate_hbm, taps_hbm, bias_hbm, skip_hbm, before_ref, in_ref, out_ref,
    y_ref, sums_ref, carry_ref, scaled_ref,
    inp_ref, raw_ref, rate_ref, taps_ref, bias_ref, skip_ref, pad_ref, delta_ref, conv_ref, sems,
):
    sources = (inp_hbm, raw_hbm, rate_hbm, taps_hbm, bias_hbm, skip_hbm)
    places = (inp_ref, raw_ref, rate_ref, taps_ref, bias_ref, skip_ref)
    copies = [
        pltpu.make_async_copy(source, place, sems.at[k])
        for k, (source, place) in enumerate(zip(sources, places))
    ]
    for copy in copies:
        copy.start()
    for copy in copies:
        copy.wait()
    length, width = inp_ref.shape
    states = rate_ref.shape[0]
    tiles = width // LANES
    for j in range(tiles):
        cols = slice(j * LANES, (j + 1) * LANES)
        pad_ref[SUB - KCONV + 1 : SUB, :] = before_ref[:, cols].astype(jnp.float32)
        pad_ref[SUB:, :] = inp_ref[:, cols].astype(jnp.float32)
        summed = jnp.broadcast_to(bias_ref[:, cols], (length, LANES))
        for k in range(KCONV):
            begin = SUB - KCONV + 1 + k
            summed = summed + taps_ref[k : k + 1, cols] * pad_ref[begin : begin + length, :]
        conv_ref[pl.ds(j, length, stride=tiles), :] = summed * jax.nn.sigmoid(summed)
        raw = raw_ref[:, cols].astype(jnp.float32)
        delta_ref[pl.ds(j, length, stride=tiles), :] = jnp.maximum(raw, 0.0) + jnp.log1p(
            jnp.exp(-jnp.abs(raw))
        )
        scaled_ref[pl.ds(j, states, stride=tiles), :] = rate_ref[:, cols] * -LOG2E

    skip = skip_ref[...]

    def step(t, carry):
        total, state = carry
        rows = pl.ds(pl.multiple_of(t * SUB, SUB), SUB)
        delta, value = delta_ref[rows, :], conv_ref[rows, :]
        total = total + delta
        out = skip * value
        after = []
        for n in range(states):
            retain = jnp.exp2(delta * scaled_ref[n * SUB : (n + 1) * SUB, :])
            fresh = in_ref[t * states + n] * value
            now = fresh + retain * (state[n] - fresh)
            out = out + out_ref[t * states + n] * now
            after.append(now)
        sums_ref[rows, :] = total
        y_ref[rows, :] = out
        return total, tuple(after)

    zero = jnp.zeros((SUB, LANES), jnp.float32)
    total, state = lax.fori_loop(0, length, step, (zero, (zero,) * states), unroll=2)
    for n in range(states):
        carry_ref[n * SUB : (n + 1) * SUB, :] = state[n]
    carry_ref[states * SUB :, :] = total


def finish_scan_kernel(
    y_ref, sums_ref, start_ref, scaled_ref, gate_hbm, out_ref, mixed_ref, full_ref, gate_ref, sem
):
    copy = pltpu.make_async_copy(gate_hbm, gate_ref, sem)
    copy.start()
    length, width = gate_ref.shape
    states = start_ref.shape[0] // SUB
    tiles = width // LANES

    def step(t, carry):
        rows = pl.ds(pl.multiple_of(t * SUB, SUB), SUB)
        total, out = sums_ref[rows, :], y_ref[rows, :]
        for n in range(states):
            part = slice(n * SUB, (n + 1) * SUB)
            kept = jnp.exp2(total * scaled_ref[part, :]) * start_ref[part, :]
            out = out + out_ref[t * states + n] * kept
        full_ref[rows, :] = out
        return carry

    lax.fori_loop(0, length, step, 0, unroll=2)
    copy.wait()
    for j in range(tiles):
        cols = slice(j * LANES, (j + 1) * LANES)
        gate = gate_ref[:, cols].astype(jnp.float32)
        gated = full_ref[pl.ds(j, length, stride=tiles), :] * (gate * jax.nn.sigmoid(gate))
        mixed_ref[:, cols] = gated.astype(mixed_ref.dtype)


def local_scan(inp, before, raw, rate, taps, bias, skip, in_flat, out_flat):
    length, width = inp.shape
    states = rate.shape[0]
    flat = jax.ShapeDtypeStruct((length * SUB, LANES), jnp.float32)
    arrays = (inp, raw, rate, taps, bias, skip)
    return pl.pallas_call(
        local_scan_kernel,
        name="local_scan",
        out_shape=(
            flat,
            flat,
            jax.ShapeDtypeStruct(((states + 1) * SUB, LANES), jnp.float32),
            jax.ShapeDtypeStruct((states * SUB, LANES), jnp.float32),
        ),
        in_specs=[HBM] * 6 + [VMEM] + [SMEM] * 2,
        out_specs=(VMEM,) * 4,
        scratch_shapes=[pltpu.VMEM(a.shape, a.dtype) for a in arrays]
        + [
            pltpu.VMEM((length + SUB, LANES), jnp.float32),
            pltpu.VMEM((length * SUB, LANES), jnp.float32),
            pltpu.VMEM((length * SUB, LANES), jnp.float32),
            pltpu.SemaphoreType.DMA((6,)),
        ],
        compiler_params=pltpu.CompilerParams(vmem_limit_bytes=58 << 20),
        cost_estimate=pl.CostEstimate(flops=8_000_000, transcendentals=2_500_000, bytes_accessed=2_000_000),
    )(*arrays, before, in_flat, out_flat)


def finish_scan(y, sums, start, scaled, gate, out_flat):
    length, width = gate.shape
    return pl.pallas_call(
        finish_scan_kernel,
        name="finish_scan",
        out_shape=jax.ShapeDtypeStruct((length, width), jnp.bfloat16),
        in_specs=[VMEM] * 4 + [HBM] + [SMEM],
        out_specs=VMEM,
        scratch_shapes=[
            pltpu.VMEM((length * SUB, LANES), jnp.float32),
            pltpu.VMEM((length, width), jnp.bfloat16),
            pltpu.SemaphoreType.DMA,
        ],
        compiler_params=pltpu.CompilerParams(vmem_limit_bytes=16 << 20),
        cost_estimate=pl.CostEstimate(flops=8_000_000, transcendentals=2_500_000, bytes_accessed=2_000_000),
    )(y, sums, start, scaled, gate, out_flat)


def entering_state(carry, scaled):
    states = scaled.shape[0] // SUB
    scaled = scaled.reshape(states, SUB, LANES)
    y, x, c = split_place(lax.axis_index("seq"))

    def parts(block):
        block = block.reshape(states + 1, SUB, LANES)
        return block[states], block[:states]

    def kept(span, state):
        return jnp.exp2(span[None] * scaled) * state

    def packed(span, state):
        return jnp.concatenate([state, span[None]], axis=0).reshape(carry.shape)

    own = parts(carry)
    other = parts(moved(carry, dc=1))
    is_first = c == 0
    first = [jnp.where(is_first, a, b) for a, b in zip(own, other)]
    last = [jnp.where(is_first, b, a) for a, b in zip(own, other)]
    chip = (first[0] + last[0], kept(last[0], first[1]) + last[1])
    start = jnp.where(is_first, 0.0, other[1])
    span = jnp.where(is_first, 0.0, other[0])

    sent = packed(*chip)
    near = [parts(moved(sent, dx=k)) for k in range(1, SIDE)]
    ahead = jnp.zeros_like(span)
    behind = jnp.zeros_like(span)
    row_state = jnp.zeros_like(chip[1])
    earlier_state = jnp.zeros_like(chip[1])
    for k in range(1, SIDE):
        got_span, got_state = near[k - 1]
        is_earlier = k <= x
        earlier_state = earlier_state + jnp.where(is_earlier, kept(ahead, got_state), 0.0)
        row_state = row_state + jnp.where(is_earlier, 0.0, kept(behind, got_state))
        ahead = ahead + jnp.where(is_earlier, got_span, 0.0)
        behind = behind + jnp.where(is_earlier, 0.0, got_span)
    row_state = row_state + kept(behind, chip[1] + kept(chip[0], earlier_state))
    row_span = ahead + chip[0] + behind
    start = start + kept(span, earlier_state)
    span = span + ahead

    sent = packed(row_span, row_state)
    far = [parts(moved(sent, dy=k)) for k in range(1, SIDE)]
    for k in range(1, SIDE):
        got_span, got_state = far[k - 1]
        is_earlier = k <= y
        start = start + jnp.where(is_earlier, kept(span, got_state), 0.0)
        span = span + jnp.where(is_earlier, got_span, 0.0)
    return start.reshape(states * SUB, LANES)


def from_before(tail):
    count = lax.axis_size("seq")
    return lax.ppermute(tail, "seq", [(i, i + 1) for i in range(count - 1)])


def around(block, ring, step):
    route = []
    for i in range(SIDE * SIDE * CORES):
        y, x, c = split_place(i)
        along_x = (ring == "inner") == (c == 0)
        dy, dx = (0, step) if along_x else (step, 0)
        route.append((i, join_place(y + dy, x + dx, c)))
    return lax.ppermute(block, "seq", route)


def added(*terms):
    return sum(t.astype(jnp.float32) for t in terms)


def expert_kernel(steps, *refs):
    count = (len(refs) - 8) // 2
    pieces, outs = refs[:count], refs[count + 6 : -2]
    gate_a, gate_b, up_a, up_b, down_a, down_b = refs[count : count + 6]
    rows_ref, acts_ref = refs[-2:]
    rows = pieces[0].shape[0]
    half = acts_ref.shape[1] // 2
    i = pl.program_id(0)

    @pl.when(i == 0)
    def _():
        for k, piece in enumerate(pieces):
            rows_ref[k * rows : (k + 1) * rows, :] = piece[...]

    @pl.when(i < steps)
    def _():
        for begin, gate, up in ((0, gate_a, up_a), (half, gate_b, up_b)):
            both = jnp.concatenate([gate[...], up[...]], axis=1)
            hidden = jnp.dot(rows_ref[...], both, preferred_element_type=jnp.float32)
            gating, upward = hidden[:, :LANES], hidden[:, LANES:]
            act = (gating * jax.nn.sigmoid(gating) * upward).astype(acts_ref.dtype)
            acts_ref[:, pl.ds(pl.multiple_of(begin + i * LANES, LANES), LANES)] = act

    @pl.when(i >= steps)
    def _():
        down = jnp.concatenate([down_a[...], down_b[...]], axis=0)
        result = jnp.dot(acts_ref[...], down, preferred_element_type=jnp.float32)
        for k, out in enumerate(outs):
            out[...] = result[k * rows : (k + 1) * rows].astype(out.dtype)


def expert(pieces, here, there):
    rows, width = pieces[0].shape
    count = len(pieces) * rows
    hidden = here[0].shape[1]
    steps = hidden // LANES
    tile = 4 * LANES
    into = pl.BlockSpec((width, LANES), lambda i: (0, jnp.minimum(i, steps - 1)))
    back = pl.BlockSpec((hidden, tile), lambda i: (0, jnp.maximum(i - steps, 0)))
    piece = pl.BlockSpec((rows, tile), lambda i: (0, jnp.maximum(i - steps, 0)))
    return pl.pallas_call(
        functools.partial(expert_kernel, steps),
        name="expert",
        grid=(steps + width // tile,),
        out_shape=(jax.ShapeDtypeStruct((rows, width), jnp.bfloat16),) * len(pieces),
        in_specs=[VMEM] * len(pieces) + [into] * 4 + [back] * 2,
        out_specs=(piece,) * len(pieces),
        scratch_shapes=[
            pltpu.VMEM((count, width), jnp.bfloat16),
            pltpu.VMEM((count, 2 * hidden), jnp.bfloat16),
        ],
        compiler_params=pltpu.CompilerParams(vmem_limit_bytes=42 << 20),
        cost_estimate=pl.CostEstimate(
            flops=12 * count * width * hidden, transcendentals=2 * count * hidden, bytes_accessed=24_000_000
        ),
    )(*pieces, here[0], there[0], here[1], there[1], here[2], there[2])


def experts_of_rows(block, here, there):
    dtype = block.dtype
    near = [block] + [around(block, "inner", k) for k in range(1, SIDE)]
    low, high = jnp.concatenate(near[:2], axis=0), jnp.concatenate(near[2:], axis=0)
    low_up = around(low, "outer", 1)
    high_down = around(high, "outer", -1)
    high_up = around(high, "outer", 1)
    low_down = around(low, "outer", -1)
    low_far = around(low_up, "outer", 1)
    high_far = around(high_down, "outer", -1)
    low_far, high_far, low, high, low_up, high_down, low_down, high_up = expert(
        [low_far, high_far, low, high, low_up, high_down, low_down, high_up], here, there
    )
    got_high_down = around(high_down, "outer", 1)
    got_low_up = around(low_up, "outer", -1)
    low_relay = around(low_far, "outer", 1)
    high_relay = around(high_far, "outer", -1)
    got_low_down = around(added(low_down, low_relay).astype(dtype), "outer", 1)
    got_high_up = around(added(high_up, high_relay).astype(dtype), "outer", -1)
    low_sum = added(low, got_low_up, got_low_down)
    high_sum = added(high, got_high_down, got_high_up)
    rows = block.shape[0]
    blocks = [low_sum[:rows], low_sum[rows:], high_sum[:rows], high_sum[rows:]]
    back = [around(blocks[k].astype(dtype), "inner", -k) for k in range(1, SIDE)]
    return added(blocks[0], *back).astype(dtype)


def project_kernel(mixed_ref, weight_ref, out_ref):
    owners, rows = out_ref.shape[:2]
    both = jnp.concatenate([weight_ref[0], weight_ref[1]], axis=1)
    result = jnp.dot(mixed_ref[...], both, preferred_element_type=jnp.float32).astype(out_ref.dtype)
    for owner in range(owners):
        out_ref[owner] = result[owner * rows : (owner + 1) * rows]


def project_part(mixed, blocks, begin, end):
    owners = lax.axis_size("exp")
    tokens, depth = mixed.shape
    rows = tokens // owners
    count = end - begin
    return pl.pallas_call(
        project_kernel,
        name="project",
        grid=(count // 2,),
        out_shape=jax.ShapeDtypeStruct((owners, rows, count * LANES), jnp.bfloat16),
        in_specs=[VMEM, pl.BlockSpec((2, depth, LANES), lambda i: (i + begin // 2, 0, 0))],
        out_specs=pl.BlockSpec((owners, rows, 2 * LANES), lambda i: (0, 0, i)),
        compiler_params=pltpu.CompilerParams(vmem_limit_bytes=56 << 20),
        cost_estimate=pl.CostEstimate(
            flops=2 * tokens * depth * count * LANES,
            transcendentals=0,
            bytes_accessed=2 * depth * count * LANES + 4 * tokens * depth,
        ),
    )(mixed, blocks)


def project(mixed, weight):
    blocks = lax.all_gather(weight, "seq")
    count = blocks.shape[0]
    begin = count * 7 // 16 // 2 * 2
    first = project_part(mixed, blocks, 0, begin)
    first = lax.psum_scatter(first, "exp", scatter_dimension=0, tiled=False)
    second = project_part(mixed, blocks, begin, count)
    second = lax.all_to_all(second, "exp", 0, 0, tiled=True)
    second = added(*(second[k] for k in range(second.shape[0])))
    return jnp.concatenate([first.astype(jnp.float32), second], axis=1)


def shards(
    mixer_input,
    gate_input,
    delta_raw,
    input_coef,
    output_coef,
    decay_rate,
    conv_weight,
    conv_bias,
    skip_gain,
    out_weight,
    residual,
    norm_gain,
    router_weight,
    expert_ids,
    gate_weight,
    up_weight,
    down_weight,
):
    length = mixer_input.shape[0]
    in_flat = input_coef.astype(jnp.float32).reshape(-1)
    out_flat = output_coef.astype(jnp.float32).reshape(-1)
    before = from_before(mixer_input[length - (KCONV - 1) :])
    y, sums, carry, scaled = local_scan(
        mixer_input,
        before,
        delta_raw,
        decay_rate,
        conv_weight,
        conv_bias.reshape(1, -1),
        skip_gain.reshape(SUB, LANES),
        in_flat,
        out_flat,
    )
    here = [w[0] for w in (gate_weight, up_weight, down_weight)]
    there = [moved(w, dc=1) for w in here]
    carry, *there = lax.optimization_barrier((carry, *there))
    start = entering_state(carry, scaled)
    mixed = finish_scan(y, sums, start, scaled, gate_input, out_flat)
    rows = residual.shape[0]
    model_width = residual.shape[1]
    projected = project(mixed, out_weight)
    hidden_state = residual.astype(jnp.float32) + projected
    scale = lax.rsqrt(jnp.mean(hidden_state * hidden_state, axis=1, keepdims=True) + 1e-06)
    normed = (hidden_state * scale * norm_gain[None, :]).astype(jnp.bfloat16)
    experts = router_weight.shape[1]
    capacity = 2 * rows // experts + 1
    logits = jnp.dot(normed, router_weight, preferred_element_type=jnp.float32)
    expert_range = jnp.arange(experts, dtype=jnp.int32)
    matches = expert_ids[:, :, None] == expert_range[None, None, :]
    chosen = jnp.sum(jnp.where(matches, logits[:, None, :], 0.0), axis=2)
    first = jax.nn.sigmoid(chosen[:, 0] - chosen[:, 1])
    flat_ids = expert_ids.reshape(-1)
    position = jnp.arange(flat_ids.shape[0], dtype=jnp.int32)
    earlier = (flat_ids[:, None] == flat_ids[None, :]) & (position[None, :] < position[:, None])
    rank = jnp.sum(earlier.astype(jnp.int32), axis=1)
    target = flat_ids * capacity + rank
    placing = (jnp.arange(experts * capacity, dtype=jnp.int32)[:, None] == target[None, :]).astype(
        jnp.bfloat16
    )
    repeated = jnp.broadcast_to(normed[:, None, :], (rows, 2, model_width)).reshape(-1, model_width)
    outgoing = (
        jnp.dot(placing, repeated, preferred_element_type=jnp.float32)
        .astype(jnp.bfloat16)
        .reshape(experts, capacity, model_width)
    )
    arrived = lax.all_to_all(outgoing, "exp", split_axis=0, concat_axis=0, tiled=True)
    flat_rows = arrived.reshape(-1, arrived.shape[2])
    summed_out = experts_of_rows(flat_rows, here, there)
    returned = lax.all_to_all(
        summed_out.reshape(arrived.shape), "exp", split_axis=0, concat_axis=0, tiled=True
    )
    flat_returned = returned.reshape(-1, model_width)
    picked = jnp.einsum(
        "sa,sd->ad", placing, flat_returned, preferred_element_type=jnp.float32
    ).reshape(rows, 2, model_width)
    moe_out = first[:, None] * picked[:, 0] + (1.0 - first)[:, None] * picked[:, 1]
    final = (hidden_state + moe_out).astype(jnp.bfloat16)
    return (mixed, final)


def solution(mesh):
    return jax.shard_map(
        shards,
        mesh=mesh,
        in_specs=(
            P("seq", "exp"),
            P("seq", "exp"),
            P("seq", "exp"),
            P("seq", None),
            P("seq", None),
            P(None, "exp"),
            P(None, "exp"),
            P("exp"),
            P("exp"),
            P("exp", "seq"),
            P(("seq", "exp"), None),
            P(),
            P(),
            P(("seq", "exp"), None),
            P("exp", None, "seq"),
            P("exp", None, "seq"),
            P("exp", "seq", None),
        ),
        out_specs=(P("seq", "exp"), P(("seq", "exp"), None)),
        check_vma=False,
    )
```

```python
import functools
import math

import jax
import jax.numpy as jnp
from jax import lax
from jax.experimental import pallas as pl
from jax.experimental.pallas import tpu as pltpu
from jax.sharding import PartitionSpec as P

KCONV = 4
LANES = 128
SUB = 8
CORES = 2
SIDE = 4
LOG2E = math.log2(math.e)
VMEM = pl.BlockSpec(memory_space=pltpu.VMEM)
SMEM = pl.BlockSpec(memory_space=pltpu.SMEM)
HBM = pl.BlockSpec(memory_space=pltpu.MemorySpace.HBM)


def split_place(place):
    return place // (SIDE * CORES), (place // CORES) % SIDE, place % CORES


def join_place(y, x, c):
    return (y % SIDE * SIDE + x % SIDE) * CORES + c % CORES


def moved(block, dy=0, dx=0, dc=0):
    route = []
    for i in range(SIDE * SIDE * CORES):
        y, x, c = split_place(i)
        route.append((i, join_place(y + dy, x + dx, c + dc)))
    return lax.ppermute(block, "seq", route)


def local_scan_kernel(
    inp_hbm, raw_hbm, rate_hbm, taps_hbm, bias_hbm, skip_hbm, before_ref, in_ref, out_ref,
    y_ref, sums_ref, carry_ref, scaled_ref,
    inp_ref, raw_ref, rate_ref, taps_ref, bias_ref, skip_ref, pad_ref, delta_ref, conv_ref, sems,
):
    sources = (inp_hbm, raw_hbm, rate_hbm, taps_hbm, bias_hbm, skip_hbm)
    places = (inp_ref, raw_ref, rate_ref, taps_ref, bias_ref, skip_ref)
    copies = [
        pltpu.make_async_copy(source, place, sems.at[k])
        for k, (source, place) in enumerate(zip(sources, places))
    ]
    for copy in copies:
        copy.start()
    for copy in copies:
        copy.wait()
    length, width = inp_ref.shape
    states = rate_ref.shape[0]
    tiles = width // LANES
    for j in range(tiles):
        cols = slice(j * LANES, (j + 1) * LANES)
        pad_ref[SUB - KCONV + 1 : SUB, :] = before_ref[:, cols].astype(jnp.float32)
        pad_ref[SUB:, :] = inp_ref[:, cols].astype(jnp.float32)
        summed = jnp.broadcast_to(bias_ref[:, cols], (length, LANES))
        for k in range(KCONV):
            begin = SUB - KCONV + 1 + k
            summed = summed + taps_ref[k : k + 1, cols] * pad_ref[begin : begin + length, :]
        conv_ref[pl.ds(j, length, stride=tiles), :] = summed * jax.nn.sigmoid(summed)
        raw = raw_ref[:, cols].astype(jnp.float32)
        delta_ref[pl.ds(j, length, stride=tiles), :] = jnp.maximum(raw, 0.0) + jnp.log1p(
            jnp.exp(-jnp.abs(raw))
        )
        scaled_ref[pl.ds(j, states, stride=tiles), :] = rate_ref[:, cols] * -LOG2E

    skip = skip_ref[...]

    def step(t, carry):
        total, state = carry
        rows = pl.ds(pl.multiple_of(t * SUB, SUB), SUB)
        delta, value = delta_ref[rows, :], conv_ref[rows, :]
        total = total + delta
        out = skip * value
        after = []
        for n in range(states):
            retain = jnp.exp2(delta * scaled_ref[n * SUB : (n + 1) * SUB, :])
            fresh = in_ref[t * states + n] * value
            now = fresh + retain * (state[n] - fresh)
            out = out + out_ref[t * states + n] * now
            after.append(now)
        sums_ref[rows, :] = total
        y_ref[rows, :] = out
        return total, tuple(after)

    zero = jnp.zeros((SUB, LANES), jnp.float32)
    total, state = lax.fori_loop(0, length, step, (zero, (zero,) * states), unroll=2)
    for n in range(states):
        carry_ref[n * SUB : (n + 1) * SUB, :] = state[n]
    carry_ref[states * SUB :, :] = total


def finish_scan_kernel(
    y_ref, sums_ref, start_ref, scaled_ref, gate_hbm, out_ref, mixed_ref, full_ref, gate_ref, sem
):
    copy = pltpu.make_async_copy(gate_hbm, gate_ref, sem)
    copy.start()
    length, width = gate_ref.shape
    states = start_ref.shape[0] // SUB
    tiles = width // LANES

    def step(t, carry):
        rows = pl.ds(pl.multiple_of(t * SUB, SUB), SUB)
        total, out = sums_ref[rows, :], y_ref[rows, :]
        for n in range(states):
            part = slice(n * SUB, (n + 1) * SUB)
            kept = jnp.exp2(total * scaled_ref[part, :]) * start_ref[part, :]
            out = out + out_ref[t * states + n] * kept
        full_ref[rows, :] = out
        return carry

    lax.fori_loop(0, length, step, 0, unroll=2)
    copy.wait()
    for j in range(tiles):
        cols = slice(j * LANES, (j + 1) * LANES)
        gate = gate_ref[:, cols].astype(jnp.float32)
        gated = full_ref[pl.ds(j, length, stride=tiles), :] * (gate * jax.nn.sigmoid(gate))
        mixed_ref[:, cols] = gated.astype(mixed_ref.dtype)


def local_scan(inp, before, raw, rate, taps, bias, skip, in_flat, out_flat):
    length, width = inp.shape
    states = rate.shape[0]
    flat = jax.ShapeDtypeStruct((length * SUB, LANES), jnp.float32)
    arrays = (inp, raw, rate, taps, bias, skip)
    return pl.pallas_call(
        local_scan_kernel,
        name="local_scan",
        out_shape=(
            flat,
            flat,
            jax.ShapeDtypeStruct(((states + 1) * SUB, LANES), jnp.float32),
            jax.ShapeDtypeStruct((states * SUB, LANES), jnp.float32),
        ),
        in_specs=[HBM] * 6 + [VMEM] + [SMEM] * 2,
        out_specs=(VMEM,) * 4,
        scratch_shapes=[pltpu.VMEM(a.shape, a.dtype) for a in arrays]
        + [
            pltpu.VMEM((length + SUB, LANES), jnp.float32),
            pltpu.VMEM((length * SUB, LANES), jnp.float32),
            pltpu.VMEM((length * SUB, LANES), jnp.float32),
            pltpu.SemaphoreType.DMA((6,)),
        ],
        compiler_params=pltpu.CompilerParams(vmem_limit_bytes=58 << 20),
        cost_estimate=pl.CostEstimate(flops=8_000_000, transcendentals=2_500_000, bytes_accessed=2_000_000),
    )(*arrays, before, in_flat, out_flat)


def finish_scan(y, sums, start, scaled, gate, out_flat):
    length, width = gate.shape
    return pl.pallas_call(
        finish_scan_kernel,
        name="finish_scan",
        out_shape=jax.ShapeDtypeStruct((length, width), jnp.bfloat16),
        in_specs=[VMEM] * 4 + [HBM] + [SMEM],
        out_specs=VMEM,
        scratch_shapes=[
            pltpu.VMEM((length * SUB, LANES), jnp.float32),
            pltpu.VMEM((length, width), jnp.bfloat16),
            pltpu.SemaphoreType.DMA,
        ],
        compiler_params=pltpu.CompilerParams(vmem_limit_bytes=16 << 20),
        cost_estimate=pl.CostEstimate(flops=8_000_000, transcendentals=2_500_000, bytes_accessed=2_000_000),
    )(y, sums, start, scaled, gate, out_flat)


def entering_state(carry, scaled):
    states = scaled.shape[0] // SUB
    scaled = scaled.reshape(states, SUB, LANES)
    y, x, c = split_place(lax.axis_index("seq"))

    def parts(block):
        block = block.reshape(states + 1, SUB, LANES)
        return block[states], block[:states]

    def kept(span, state):
        return jnp.exp2(span[None] * scaled) * state

    def packed(span, state):
        return jnp.concatenate([state, span[None]], axis=0).reshape(carry.shape)

    own = parts(carry)
    other = parts(moved(carry, dc=1))
    is_first = c == 0
    first = [jnp.where(is_first, a, b) for a, b in zip(own, other)]
    last = [jnp.where(is_first, b, a) for a, b in zip(own, other)]
    chip = (first[0] + last[0], kept(last[0], first[1]) + last[1])
    start = jnp.where(is_first, 0.0, other[1])
    span = jnp.where(is_first, 0.0, other[0])

    sent = packed(*chip)
    near = [parts(moved(sent, dx=k)) for k in range(1, SIDE)]
    ahead = jnp.zeros_like(span)
    behind = jnp.zeros_like(span)
    row_state = jnp.zeros_like(chip[1])
    earlier_state = jnp.zeros_like(chip[1])
    for k in range(1, SIDE):
        got_span, got_state = near[k - 1]
        is_earlier = k <= x
        earlier_state = earlier_state + jnp.where(is_earlier, kept(ahead, got_state), 0.0)
        row_state = row_state + jnp.where(is_earlier, 0.0, kept(behind, got_state))
        ahead = ahead + jnp.where(is_earlier, got_span, 0.0)
        behind = behind + jnp.where(is_earlier, 0.0, got_span)
    row_state = row_state + kept(behind, chip[1] + kept(chip[0], earlier_state))
    row_span = ahead + chip[0] + behind
    start = start + kept(span, earlier_state)
    span = span + ahead

    sent = packed(row_span, row_state)
    far = [parts(moved(sent, dy=k)) for k in range(1, SIDE)]
    for k in range(1, SIDE):
        got_span, got_state = far[k - 1]
        is_earlier = k <= y
        start = start + jnp.where(is_earlier, kept(span, got_state), 0.0)
        span = span + jnp.where(is_earlier, got_span, 0.0)
    return start.reshape(states * SUB, LANES)


def from_before(tail):
    count = lax.axis_size("seq")
    return lax.ppermute(tail, "seq", [(i, i + 1) for i in range(count - 1)])


def around(block, ring, step):
    route = []
    for i in range(SIDE * SIDE * CORES):
        y, x, c = split_place(i)
        along_x = (ring == "inner") == (c == 0)
        dy, dx = (0, step) if along_x else (step, 0)
        route.append((i, join_place(y + dy, x + dx, c)))
    return lax.ppermute(block, "seq", route)


def added(*terms):
    return sum(t.astype(jnp.float32) for t in terms)


def expert_kernel(steps, *refs):
    count = (len(refs) - 8) // 2
    pieces, outs = refs[:count], refs[count + 6 : -2]
    gate_a, gate_b, up_a, up_b, down_a, down_b = refs[count : count + 6]
    rows_ref, acts_ref = refs[-2:]
    rows = pieces[0].shape[0]
    half = acts_ref.shape[1] // 2
    i = pl.program_id(0)

    @pl.when(i == 0)
    def _():
        for k, piece in enumerate(pieces):
            rows_ref[k * rows : (k + 1) * rows, :] = piece[...]

    @pl.when(i < steps)
    def _():
        for begin, gate, up in ((0, gate_a, up_a), (half, gate_b, up_b)):
            both = jnp.concatenate([gate[...], up[...]], axis=1)
            hidden = jnp.dot(rows_ref[...], both, preferred_element_type=jnp.float32)
            gating, upward = hidden[:, :LANES], hidden[:, LANES:]
            act = (gating * jax.nn.sigmoid(gating) * upward).astype(acts_ref.dtype)
            acts_ref[:, pl.ds(pl.multiple_of(begin + i * LANES, LANES), LANES)] = act

    @pl.when(i >= steps)
    def _():
        down = jnp.concatenate([down_a[...], down_b[...]], axis=0)
        result = jnp.dot(acts_ref[...], down, preferred_element_type=jnp.float32)
        for k, out in enumerate(outs):
            out[...] = result[k * rows : (k + 1) * rows].astype(out.dtype)


def expert(pieces, here, there):
    rows, width = pieces[0].shape
    count = len(pieces) * rows
    hidden = here[0].shape[1]
    steps = hidden // LANES
    tile = 4 * LANES
    into = pl.BlockSpec((width, LANES), lambda i: (0, jnp.minimum(i, steps - 1)))
    back = pl.BlockSpec((hidden, tile), lambda i: (0, jnp.maximum(i - steps, 0)))
    piece = pl.BlockSpec((rows, tile), lambda i: (0, jnp.maximum(i - steps, 0)))
    return pl.pallas_call(
        functools.partial(expert_kernel, steps),
        name="expert",
        grid=(steps + width // tile,),
        out_shape=(jax.ShapeDtypeStruct((rows, width), jnp.bfloat16),) * len(pieces),
        in_specs=[VMEM] * len(pieces) + [into] * 4 + [back] * 2,
        out_specs=(piece,) * len(pieces),
        scratch_shapes=[
            pltpu.VMEM((count, width), jnp.bfloat16),
            pltpu.VMEM((count, 2 * hidden), jnp.bfloat16),
        ],
        compiler_params=pltpu.CompilerParams(vmem_limit_bytes=42 << 20),
        cost_estimate=pl.CostEstimate(
            flops=12 * count * width * hidden, transcendentals=2 * count * hidden, bytes_accessed=24_000_000
        ),
    )(*pieces, here[0], there[0], here[1], there[1], here[2], there[2])


def experts_of_rows(block, here, there):
    dtype = block.dtype
    half = block.shape[1] // 2
    after, before = around(block, "inner", 1), around(block, "inner", -1)
    across = jnp.concatenate(
        [around(after[:, :half], "inner", 1), around(before[:, half:], "inner", -1)], axis=1
    )
    near = [block, after, across, before]
    low, high = jnp.concatenate(near[:2], axis=0), jnp.concatenate(near[2:], axis=0)
    low_up = around(low, "outer", 1)
    high_down = around(high, "outer", -1)
    high_up = around(high, "outer", 1)
    low_down = around(low, "outer", -1)
    low_far = around(low_up, "outer", 1)
    high_far = around(high_down, "outer", -1)
    low_far, high_far, low, high, low_up, high_down, low_down, high_up = expert(
        [low_far, high_far, low, high, low_up, high_down, low_down, high_up], here, there
    )
    got_high_down = around(high_down, "outer", 1)
    got_low_up = around(low_up, "outer", -1)
    low_relay = around(low_far, "outer", 1)
    high_relay = around(high_far, "outer", -1)
    got_low_down = around(added(low_down, low_relay).astype(dtype), "outer", 1)
    got_high_up = around(added(high_up, high_relay).astype(dtype), "outer", -1)
    low_sum = added(low, got_low_up, got_low_down)
    high_sum = added(high, got_high_down, got_high_up)
    rows = block.shape[0]
    blocks = [low_sum[:rows], low_sum[rows:], high_sum[:rows], high_sum[rows:]]
    back = [around(blocks[k].astype(dtype), "inner", -k) for k in range(1, SIDE)]
    return added(blocks[0], *back).astype(dtype)


def project_kernel(mixed_ref, *refs):
    blocks, out_ref = refs[:-1], refs[-1]
    owners, rows = out_ref.shape[:2]
    weight = jnp.concatenate([block[...] for block in blocks], axis=1)
    result = jnp.dot(mixed_ref[...], weight, preferred_element_type=jnp.float32).astype(out_ref.dtype)
    for owner in range(owners):
        out_ref[owner] = result[owner * rows : (owner + 1) * rows]


def project(mixed, weight):
    blocks = lax.all_gather(weight, "seq")
    owners = lax.axis_size("exp")
    tokens, depth = mixed.shape
    count = blocks.shape[0]
    group = SIDE
    rows = tokens // owners
    views = [pl.BlockSpec((None, depth, LANES), lambda i, q=q: (group * i + q, 0, 0)) for q in range(group)]
    terms = pl.pallas_call(
        project_kernel,
        name="project",
        grid=(count // group,),
        out_shape=jax.ShapeDtypeStruct((owners, rows, count * LANES), jnp.bfloat16),
        in_specs=[VMEM] + views,
        out_specs=pl.BlockSpec((owners, rows, group * LANES), lambda i: (0, 0, i)),
        compiler_params=pltpu.CompilerParams(vmem_limit_bytes=56 << 20),
        cost_estimate=pl.CostEstimate(
            flops=2 * tokens * depth * count * LANES, transcendentals=0, bytes_accessed=10_000_000
        ),
    )(mixed, *([blocks] * group))
    terms = lax.all_to_all(terms, "exp", 0, 0, tiled=True)
    return added(*(terms[k] for k in range(owners)))


def shards(
    mixer_input,
    gate_input,
    delta_raw,
    input_coef,
    output_coef,
    decay_rate,
    conv_weight,
    conv_bias,
    skip_gain,
    out_weight,
    residual,
    norm_gain,
    router_weight,
    expert_ids,
    gate_weight,
    up_weight,
    down_weight,
):
    length = mixer_input.shape[0]
    in_flat = input_coef.astype(jnp.float32).reshape(-1)
    out_flat = output_coef.astype(jnp.float32).reshape(-1)
    before = from_before(mixer_input[length - (KCONV - 1) :])
    y, sums, carry, scaled = local_scan(
        mixer_input,
        before,
        delta_raw,
        decay_rate,
        conv_weight,
        conv_bias.reshape(1, -1),
        skip_gain.reshape(SUB, LANES),
        in_flat,
        out_flat,
    )
    here = [w[0] for w in (gate_weight, up_weight, down_weight)]
    there = [moved(w, dc=1) for w in here]
    carry, *there = lax.optimization_barrier((carry, *there))
    start = entering_state(carry, scaled)
    mixed = finish_scan(y, sums, start, scaled, gate_input, out_flat)
    rows = residual.shape[0]
    model_width = residual.shape[1]
    projected = project(mixed, out_weight)
    hidden_state = residual.astype(jnp.float32) + projected
    scale = lax.rsqrt(jnp.mean(hidden_state * hidden_state, axis=1, keepdims=True) + 1e-06)
    normed = (hidden_state * scale * norm_gain[None, :]).astype(jnp.bfloat16)
    experts = router_weight.shape[1]
    capacity = 2 * rows // experts + 1
    logits = jnp.dot(normed, router_weight, preferred_element_type=jnp.float32)
    expert_range = jnp.arange(experts, dtype=jnp.int32)
    matches = expert_ids[:, :, None] == expert_range[None, None, :]
    chosen = jnp.sum(jnp.where(matches, logits[:, None, :], 0.0), axis=2)
    first = jax.nn.sigmoid(chosen[:, 0] - chosen[:, 1])
    flat_ids = expert_ids.reshape(-1)
    position = jnp.arange(flat_ids.shape[0], dtype=jnp.int32)
    earlier = (flat_ids[:, None] == flat_ids[None, :]) & (position[None, :] < position[:, None])
    rank = jnp.sum(earlier.astype(jnp.int32), axis=1)
    target = flat_ids * capacity + rank
    placing = (jnp.arange(experts * capacity, dtype=jnp.int32)[:, None] == target[None, :]).astype(
        jnp.bfloat16
    )
    repeated = jnp.broadcast_to(normed[:, None, :], (rows, 2, model_width)).reshape(-1, model_width)
    outgoing = jnp.dot(placing, repeated, preferred_element_type=jnp.float32).astype(jnp.bfloat16)
    outgoing = outgoing.reshape(experts, -1, LANES)
    arrived = lax.all_to_all(outgoing, "exp", split_axis=0, concat_axis=0, tiled=True)
    flat_rows = arrived.reshape(-1, model_width)
    summed_out = experts_of_rows(flat_rows, here, there)
    returned = lax.all_to_all(
        summed_out.reshape(arrived.shape), "exp", split_axis=0, concat_axis=0, tiled=True
    )
    flat_returned = returned.reshape(-1, model_width)
    picked = jnp.einsum(
        "sa,sd->ad", placing, flat_returned, preferred_element_type=jnp.float32
    ).reshape(rows, 2, model_width)
    moe_out = first[:, None] * picked[:, 0] + (1.0 - first)[:, None] * picked[:, 1]
    final = (hidden_state + moe_out).astype(jnp.bfloat16)
    return (mixed, final)


def solution(mesh):
    return jax.shard_map(
        shards,
        mesh=mesh,
        in_specs=(
            P("seq", "exp"),
            P("seq", "exp"),
            P("seq", "exp"),
            P("seq", None),
            P("seq", None),
            P(None, "exp"),
            P(None, "exp"),
            P("exp"),
            P("exp"),
            P("exp", "seq"),
            P(("seq", "exp"), None),
            P(),
            P(),
            P(("seq", "exp"), None),
            P("exp", None, "seq"),
            P("exp", None, "seq"),
            P("exp", "seq", None),
        ),
        out_specs=(P("seq", "exp"), P(("seq", "exp"), None)),
        check_vma=False,
    )
```

```python
import functools
import math

import jax
import jax.numpy as jnp
from jax import lax
from jax.experimental import pallas as pl
from jax.experimental.pallas import tpu as pltpu
from jax.sharding import PartitionSpec as P

KCONV = 4
LANES = 128
SUB = 8
CORES = 2
SIDE = 4
LOG2E = math.log2(math.e)
VMEM = pl.BlockSpec(memory_space=pltpu.VMEM)
SMEM = pl.BlockSpec(memory_space=pltpu.SMEM)
HBM = pl.BlockSpec(memory_space=pltpu.MemorySpace.HBM)


def split_place(place):
    return place // (SIDE * CORES), (place // CORES) % SIDE, place % CORES


def join_place(y, x, c):
    return (y % SIDE * SIDE + x % SIDE) * CORES + c % CORES


def moved(block, dy=0, dx=0, dc=0):
    route = []
    for i in range(SIDE * SIDE * CORES):
        y, x, c = split_place(i)
        route.append((i, join_place(y + dy, x + dx, c + dc)))
    return lax.ppermute(block, "seq", route)


def local_scan_kernel(
    inp_hbm, raw_hbm, rate_hbm, taps_hbm, bias_hbm, skip_hbm, before_ref, in_ref, out_ref,
    y_ref, sums_ref, carry_ref, scaled_ref,
    inp_ref, raw_ref, rate_ref, taps_ref, bias_ref, skip_ref, pad_ref, delta_ref, conv_ref, sems,
):
    sources = (inp_hbm, raw_hbm, rate_hbm, taps_hbm, bias_hbm, skip_hbm)
    places = (inp_ref, raw_ref, rate_ref, taps_ref, bias_ref, skip_ref)
    copies = [
        pltpu.make_async_copy(source, place, sems.at[k])
        for k, (source, place) in enumerate(zip(sources, places))
    ]
    for copy in copies:
        copy.start()
    for copy in copies:
        copy.wait()
    length, width = inp_ref.shape
    states = rate_ref.shape[0]
    tiles = width // LANES
    for j in range(tiles):
        cols = slice(j * LANES, (j + 1) * LANES)
        pad_ref[SUB - KCONV + 1 : SUB, :] = before_ref[:, cols].astype(jnp.float32)
        pad_ref[SUB:, :] = inp_ref[:, cols].astype(jnp.float32)
        summed = jnp.broadcast_to(bias_ref[:, cols], (length, LANES))
        for k in range(KCONV):
            begin = SUB - KCONV + 1 + k
            summed = summed + taps_ref[k : k + 1, cols] * pad_ref[begin : begin + length, :]
        conv_ref[pl.ds(j, length, stride=tiles), :] = summed * jax.nn.sigmoid(summed)
        raw = raw_ref[:, cols].astype(jnp.float32)
        delta_ref[pl.ds(j, length, stride=tiles), :] = jnp.maximum(raw, 0.0) + jnp.log1p(
            jnp.exp(-jnp.abs(raw))
        )
        scaled_ref[pl.ds(j, states, stride=tiles), :] = rate_ref[:, cols] * -LOG2E

    skip = skip_ref[...]

    def step(t, carry):
        total, state = carry
        rows = pl.ds(pl.multiple_of(t * SUB, SUB), SUB)
        delta, value = delta_ref[rows, :], conv_ref[rows, :]
        total = total + delta
        out = skip * value
        after = []
        for n in range(states):
            retain = jnp.exp2(delta * scaled_ref[n * SUB : (n + 1) * SUB, :])
            fresh = in_ref[t * states + n] * value
            now = fresh + retain * (state[n] - fresh)
            out = out + out_ref[t * states + n] * now
            after.append(now)
        sums_ref[rows, :] = total
        y_ref[rows, :] = out
        return total, tuple(after)

    zero = jnp.zeros((SUB, LANES), jnp.float32)
    total, state = lax.fori_loop(0, length, step, (zero, (zero,) * states), unroll=2)
    for n in range(states):
        carry_ref[n * SUB : (n + 1) * SUB, :] = state[n]
    carry_ref[states * SUB :, :] = total


def finish_scan_kernel(
    y_ref, sums_ref, start_ref, scaled_ref, gate_hbm, out_ref, mixed_ref, full_ref, gate_ref, sem
):
    copy = pltpu.make_async_copy(gate_hbm, gate_ref, sem)
    copy.start()
    length, width = gate_ref.shape
    states = start_ref.shape[0] // SUB
    tiles = width // LANES

    def step(t, carry):
        rows = pl.ds(pl.multiple_of(t * SUB, SUB), SUB)
        total, out = sums_ref[rows, :], y_ref[rows, :]
        for n in range(states):
            part = slice(n * SUB, (n + 1) * SUB)
            kept = jnp.exp2(total * scaled_ref[part, :]) * start_ref[part, :]
            out = out + out_ref[t * states + n] * kept
        full_ref[rows, :] = out
        return carry

    lax.fori_loop(0, length, step, 0, unroll=2)
    copy.wait()
    for j in range(tiles):
        cols = slice(j * LANES, (j + 1) * LANES)
        gate = gate_ref[:, cols].astype(jnp.float32)
        gated = full_ref[pl.ds(j, length, stride=tiles), :] * (gate * jax.nn.sigmoid(gate))
        mixed_ref[:, cols] = gated.astype(mixed_ref.dtype)


def local_scan(inp, before, raw, rate, taps, bias, skip, in_flat, out_flat):
    length, width = inp.shape
    states = rate.shape[0]
    flat = jax.ShapeDtypeStruct((length * SUB, LANES), jnp.float32)
    arrays = (inp, raw, rate, taps, bias, skip)
    return pl.pallas_call(
        local_scan_kernel,
        name="local_scan",
        out_shape=(
            flat,
            flat,
            jax.ShapeDtypeStruct(((states + 1) * SUB, LANES), jnp.float32),
            jax.ShapeDtypeStruct((states * SUB, LANES), jnp.float32),
        ),
        in_specs=[HBM] * 6 + [VMEM] + [SMEM] * 2,
        out_specs=(VMEM,) * 4,
        scratch_shapes=[pltpu.VMEM(a.shape, a.dtype) for a in arrays]
        + [
            pltpu.VMEM((length + SUB, LANES), jnp.float32),
            pltpu.VMEM((length * SUB, LANES), jnp.float32),
            pltpu.VMEM((length * SUB, LANES), jnp.float32),
            pltpu.SemaphoreType.DMA((6,)),
        ],
        compiler_params=pltpu.CompilerParams(vmem_limit_bytes=58 << 20),
        cost_estimate=pl.CostEstimate(flops=8_000_000, transcendentals=2_500_000, bytes_accessed=2_000_000),
    )(*arrays, before, in_flat, out_flat)


def finish_scan(y, sums, start, scaled, gate, out_flat):
    length, width = gate.shape
    return pl.pallas_call(
        finish_scan_kernel,
        name="finish_scan",
        out_shape=jax.ShapeDtypeStruct((length, width), jnp.bfloat16),
        in_specs=[VMEM] * 4 + [HBM] + [SMEM],
        out_specs=VMEM,
        scratch_shapes=[
            pltpu.VMEM((length * SUB, LANES), jnp.float32),
            pltpu.VMEM((length, width), jnp.bfloat16),
            pltpu.SemaphoreType.DMA,
        ],
        compiler_params=pltpu.CompilerParams(vmem_limit_bytes=16 << 20),
        cost_estimate=pl.CostEstimate(flops=8_000_000, transcendentals=2_500_000, bytes_accessed=2_000_000),
    )(y, sums, start, scaled, gate, out_flat)


def entering_state(carry, scaled):
    states = scaled.shape[0] // SUB
    scaled = scaled.reshape(states, SUB, LANES)
    y, x, c = split_place(lax.axis_index("seq"))

    def parts(block):
        block = block.reshape(states + 1, SUB, LANES)
        return block[states], block[:states]

    def kept(span, state):
        return jnp.exp2(span[None] * scaled) * state

    def packed(span, state):
        return jnp.concatenate([state, span[None]], axis=0).reshape(carry.shape)

    own = parts(carry)
    other = parts(moved(carry, dc=1))
    is_first = c == 0
    first = [jnp.where(is_first, a, b) for a, b in zip(own, other)]
    last = [jnp.where(is_first, b, a) for a, b in zip(own, other)]
    chip = (first[0] + last[0], kept(last[0], first[1]) + last[1])
    start = jnp.where(is_first, 0.0, other[1])
    span = jnp.where(is_first, 0.0, other[0])

    sent = packed(*chip)
    near = [parts(moved(sent, dx=k)) for k in range(1, SIDE)]
    ahead = jnp.zeros_like(span)
    behind = jnp.zeros_like(span)
    row_state = jnp.zeros_like(chip[1])
    earlier_state = jnp.zeros_like(chip[1])
    for k in range(1, SIDE):
        got_span, got_state = near[k - 1]
        is_earlier = k <= x
        earlier_state = earlier_state + jnp.where(is_earlier, kept(ahead, got_state), 0.0)
        row_state = row_state + jnp.where(is_earlier, 0.0, kept(behind, got_state))
        ahead = ahead + jnp.where(is_earlier, got_span, 0.0)
        behind = behind + jnp.where(is_earlier, 0.0, got_span)
    row_state = row_state + kept(behind, chip[1] + kept(chip[0], earlier_state))
    row_span = ahead + chip[0] + behind
    start = start + kept(span, earlier_state)
    span = span + ahead

    sent = packed(row_span, row_state)
    far = [parts(moved(sent, dy=k)) for k in range(1, SIDE)]
    for k in range(1, SIDE):
        got_span, got_state = far[k - 1]
        is_earlier = k <= y
        start = start + jnp.where(is_earlier, kept(span, got_state), 0.0)
        span = span + jnp.where(is_earlier, got_span, 0.0)
    return start.reshape(states * SUB, LANES)


def from_before(tail):
    count = lax.axis_size("seq")
    return lax.ppermute(tail, "seq", [(i, i + 1) for i in range(count - 1)])


def around(block, ring, step):
    route = []
    for i in range(SIDE * SIDE * CORES):
        y, x, c = split_place(i)
        along_x = (ring == "inner") == (c == 0)
        dy, dx = (0, step) if along_x else (step, 0)
        route.append((i, join_place(y + dy, x + dx, c)))
    return lax.ppermute(block, "seq", route)


def added(*terms):
    return sum(t.astype(jnp.float32) for t in terms)


def expert_in_kernel(*refs):
    pieces, (gate_a, gate_b, up_a, up_b, act_a, act_b, rows_ref) = refs[:-7], refs[-7:]
    rows = pieces[0].shape[0]

    @pl.when(pl.program_id(0) == 0)
    def _():
        for k, piece in enumerate(pieces):
            rows_ref[k * rows : (k + 1) * rows, :] = piece[...]

    for gate, up, act in ((gate_a, up_a, act_a), (gate_b, up_b, act_b)):
        both = jnp.concatenate([gate[...], up[...]], axis=1)
        hidden = jnp.dot(rows_ref[...], both, preferred_element_type=jnp.float32)
        gating, upward = hidden[:, :LANES], hidden[:, LANES:]
        act[...] = (gating * jax.nn.sigmoid(gating) * upward).astype(act.dtype)


def expert_in(pieces, here, there):
    rows, width = pieces[0].shape
    count = len(pieces) * rows
    hidden = here[0].shape[1]
    weight = pl.BlockSpec((width, LANES), lambda i: (0, i))
    act = pl.BlockSpec((count, LANES), lambda i: (0, i))
    return pl.pallas_call(
        expert_in_kernel,
        name="expert_in",
        grid=(hidden // LANES,),
        out_shape=(jax.ShapeDtypeStruct((count, hidden), jnp.bfloat16),) * 2,
        in_specs=[VMEM] * len(pieces) + [weight] * 4,
        out_specs=(act, act),
        scratch_shapes=[pltpu.VMEM((count, width), jnp.bfloat16)],
        compiler_params=pltpu.CompilerParams(vmem_limit_bytes=42 << 20),
        cost_estimate=pl.CostEstimate(
            flops=8 * count * width * hidden, transcendentals=2 * count * hidden, bytes_accessed=16_000_000
        ),
    )(*pieces, here[0], there[0], here[1], there[1])


def expert_out_kernel(places, rows, *refs):
    acts, (down_a, down_b) = refs[:4], refs[4:6]
    outs, acts_ref = refs[6:-1], refs[-1]
    hidden = down_a.shape[0]

    @pl.when(pl.program_id(0) == 0)
    def _():
        for k, (part, begin) in enumerate(places):
            for side in range(2):
                block = acts[2 * part + side][begin * rows : (begin + 1) * rows, :]
                acts_ref[k * rows : (k + 1) * rows, side * hidden : (side + 1) * hidden] = block

    down = jnp.concatenate([down_a[...], down_b[...]], axis=0)
    result = jnp.dot(acts_ref[...], down, preferred_element_type=jnp.float32)
    for k, out in enumerate(outs):
        out[...] = result[k * rows : (k + 1) * rows].astype(out.dtype)


def expert_out(places, rows, acts, here, there):
    hidden, width = here[2].shape
    count = len(places) * rows
    tile = 8 * LANES
    weight = pl.BlockSpec((hidden, tile), lambda i: (0, i))
    piece = pl.BlockSpec((rows, tile), lambda i: (0, i))
    return pl.pallas_call(
        functools.partial(expert_out_kernel, places, rows),
        name="expert_out",
        grid=(width // tile,),
        out_shape=(jax.ShapeDtypeStruct((rows, width), jnp.bfloat16),) * len(places),
        in_specs=[VMEM] * 4 + [weight] * 2,
        out_specs=(piece,) * len(places),
        scratch_shapes=[pltpu.VMEM((count, 2 * hidden), jnp.bfloat16)],
        compiler_params=pltpu.CompilerParams(vmem_limit_bytes=42 << 20),
        cost_estimate=pl.CostEstimate(
            flops=4 * count * width * hidden, transcendentals=0, bytes_accessed=9_000_000
        ),
    )(*acts, here[2], there[2])


def experts_of_rows(block, here, there):
    dtype = block.dtype
    half = block.shape[1] // 2
    after, before = around(block, "inner", 1), around(block, "inner", -1)
    across = jnp.concatenate(
        [around(after[:, :half], "inner", 1), around(before[:, half:], "inner", -1)], axis=1
    )
    near = [block, after, across, before]
    low, high = jnp.concatenate(near[:2], axis=0), jnp.concatenate(near[2:], axis=0)
    low_up = around(low, "outer", 1)
    high_down = around(high, "outer", -1)
    high_up = around(high, "outer", 1)
    low_down = around(low, "outer", -1)
    low_far = around(low_up, "outer", 1)
    high_far = around(high_down, "outer", -1)
    acts = expert_in([low, high, low_up, high_down], here, there)
    acts = [*acts, *expert_in([low_far, high_far, low_down, high_up], here, there)]
    rows = low.shape[0]
    low_far, high_far, low_up, high_down = expert_out(((1, 0), (1, 1), (0, 2), (0, 3)), rows, acts, here, there)
    got_high_down = around(high_down, "outer", 1)
    got_low_up = around(low_up, "outer", -1)
    low, high, low_down, high_up = expert_out(((0, 0), (0, 1), (1, 2), (1, 3)), rows, acts, here, there)
    low_relay = around(low_far, "outer", 1)
    high_relay = around(high_far, "outer", -1)
    got_low_down = around(added(low_down, low_relay).astype(dtype), "outer", 1)
    got_high_up = around(added(high_up, high_relay).astype(dtype), "outer", -1)
    low_sum = added(low, got_low_up, got_low_down)
    high_sum = added(high, got_high_down, got_high_up)
    rows = block.shape[0]
    blocks = [low_sum[:rows], low_sum[rows:], high_sum[:rows], high_sum[rows:]]
    back = [around(blocks[k].astype(dtype), "inner", -k) for k in range(1, SIDE)]
    return added(blocks[0], *back).astype(dtype)


def project_kernel(mixed_ref, *refs):
    blocks, out_ref = refs[:-1], refs[-1]
    owners, rows = out_ref.shape[:2]
    weight = jnp.concatenate([block[...] for block in blocks], axis=1)
    result = jnp.dot(mixed_ref[...], weight, preferred_element_type=jnp.float32).astype(out_ref.dtype)
    for owner in range(owners):
        out_ref[owner] = result[owner * rows : (owner + 1) * rows]


def project(mixed, weight):
    blocks = lax.all_gather(weight, "seq")
    owners = lax.axis_size("exp")
    tokens, depth = mixed.shape
    count = blocks.shape[0]
    group = SIDE
    rows = tokens // owners
    views = [pl.BlockSpec((None, depth, LANES), lambda i, q=q: (group * i + q, 0, 0)) for q in range(group)]
    terms = pl.pallas_call(
        project_kernel,
        name="project",
        grid=(count // group,),
        out_shape=jax.ShapeDtypeStruct((owners, rows, count * LANES), jnp.bfloat16),
        in_specs=[VMEM] + views,
        out_specs=pl.BlockSpec((owners, rows, group * LANES), lambda i: (0, 0, i)),
        compiler_params=pltpu.CompilerParams(vmem_limit_bytes=56 << 20),
        cost_estimate=pl.CostEstimate(
            flops=2 * tokens * depth * count * LANES, transcendentals=0, bytes_accessed=10_000_000
        ),
    )(mixed, *([blocks] * group))
    terms = lax.all_to_all(terms, "exp", 0, 0, tiled=True)
    return added(*(terms[k] for k in range(owners)))


def shards(
    mixer_input,
    gate_input,
    delta_raw,
    input_coef,
    output_coef,
    decay_rate,
    conv_weight,
    conv_bias,
    skip_gain,
    out_weight,
    residual,
    norm_gain,
    router_weight,
    expert_ids,
    gate_weight,
    up_weight,
    down_weight,
):
    length = mixer_input.shape[0]
    in_flat = input_coef.astype(jnp.float32).reshape(-1)
    out_flat = output_coef.astype(jnp.float32).reshape(-1)
    before = from_before(mixer_input[length - (KCONV - 1) :])
    y, sums, carry, scaled = local_scan(
        mixer_input,
        before,
        delta_raw,
        decay_rate,
        conv_weight,
        conv_bias.reshape(1, -1),
        skip_gain.reshape(SUB, LANES),
        in_flat,
        out_flat,
    )
    here = [w[0] for w in (gate_weight, up_weight, down_weight)]
    there = [moved(w, dc=1) for w in here]
    carry, *there = lax.optimization_barrier((carry, *there))
    start = entering_state(carry, scaled)
    mixed = finish_scan(y, sums, start, scaled, gate_input, out_flat)
    rows = residual.shape[0]
    model_width = residual.shape[1]
    experts = router_weight.shape[1]
    capacity = 2 * rows // experts + 1
    expert_range = jnp.arange(experts, dtype=jnp.int32)
    flat_ids = expert_ids.reshape(-1)
    position = jnp.arange(flat_ids.shape[0], dtype=jnp.int32)
    earlier = (flat_ids[:, None] == flat_ids[None, :]) & (position[None, :] < position[:, None])
    rank = jnp.sum(earlier.astype(jnp.int32), axis=1)
    target = flat_ids * capacity + rank
    mixed, target = lax.optimization_barrier((mixed, target))
    projected = project(mixed, out_weight)
    hidden_state = residual.astype(jnp.float32) + projected
    scale = lax.rsqrt(jnp.mean(hidden_state * hidden_state, axis=1, keepdims=True) + 1e-06)
    normed = (hidden_state * scale * norm_gain[None, :]).astype(jnp.bfloat16)
    logits = jnp.dot(normed, router_weight, preferred_element_type=jnp.float32)
    matches = expert_ids[:, :, None] == expert_range[None, None, :]
    chosen = jnp.sum(jnp.where(matches, logits[:, None, :], 0.0), axis=2)
    first = jax.nn.sigmoid(chosen[:, 0] - chosen[:, 1])
    placing = (jnp.arange(experts * capacity, dtype=jnp.int32)[:, None] == target[None, :]).astype(
        jnp.bfloat16
    )
    repeated = jnp.broadcast_to(normed[:, None, :], (rows, 2, model_width)).reshape(-1, model_width)
    outgoing = jnp.dot(placing, repeated, preferred_element_type=jnp.float32).astype(jnp.bfloat16)
    outgoing = outgoing.reshape(experts, -1, LANES)
    arrived = lax.all_to_all(outgoing, "exp", split_axis=0, concat_axis=0, tiled=True)
    flat_rows = arrived.reshape(-1, model_width)
    summed_out = experts_of_rows(flat_rows, here, there)
    returned = lax.all_to_all(
        summed_out.reshape(arrived.shape), "exp", split_axis=0, concat_axis=0, tiled=True
    )
    flat_returned = returned.reshape(-1, model_width)
    picked = jnp.einsum(
        "sa,sd->ad", placing, flat_returned, preferred_element_type=jnp.float32
    ).reshape(rows, 2, model_width)
    moe_out = first[:, None] * picked[:, 0] + (1.0 - first)[:, None] * picked[:, 1]
    final = (hidden_state + moe_out).astype(jnp.bfloat16)
    return (mixed, final)


def solution(mesh):
    return jax.shard_map(
        shards,
        mesh=mesh,
        in_specs=(
            P("seq", "exp"),
            P("seq", "exp"),
            P("seq", "exp"),
            P("seq", None),
            P("seq", None),
            P(None, "exp"),
            P(None, "exp"),
            P("exp"),
            P("exp"),
            P("exp", "seq"),
            P(("seq", "exp"), None),
            P(),
            P(),
            P(("seq", "exp"), None),
            P("exp", None, "seq"),
            P("exp", None, "seq"),
            P("exp", "seq", None),
        ),
        out_specs=(P("seq", "exp"), P(("seq", "exp"), None)),
        check_vma=False,
    )
```

```python
import functools
import math

import jax
import jax.numpy as jnp
from jax import lax
from jax.experimental import pallas as pl
from jax.experimental.pallas import tpu as pltpu
from jax.sharding import PartitionSpec as P

KCONV = 4
LANES = 128
SUB = 8
CORES = 2
SIDE = 4
LOG2E = math.log2(math.e)
VMEM = pl.BlockSpec(memory_space=pltpu.VMEM)
SMEM = pl.BlockSpec(memory_space=pltpu.SMEM)
HBM = pl.BlockSpec(memory_space=pltpu.MemorySpace.HBM)


def split_place(place):
    return place // (SIDE * CORES), (place // CORES) % SIDE, place % CORES


def join_place(y, x, c):
    return (y % SIDE * SIDE + x % SIDE) * CORES + c % CORES


def moved(block, dy=0, dx=0, dc=0):
    route = []
    for i in range(SIDE * SIDE * CORES):
        y, x, c = split_place(i)
        route.append((i, join_place(y + dy, x + dx, c + dc)))
    return lax.ppermute(block, "seq", route)


def local_scan_kernel(
    inp_hbm, raw_hbm, rate_hbm, taps_hbm, bias_hbm, skip_hbm, before_ref, in_ref, out_ref,
    y_ref, sums_ref, carry_ref, scaled_ref,
    inp_ref, raw_ref, rate_ref, taps_ref, bias_ref, skip_ref, pad_ref, delta_ref, conv_ref, sems,
):
    sources = (inp_hbm, raw_hbm, rate_hbm, taps_hbm, bias_hbm, skip_hbm)
    places = (inp_ref, raw_ref, rate_ref, taps_ref, bias_ref, skip_ref)
    copies = [
        pltpu.make_async_copy(source, place, sems.at[k])
        for k, (source, place) in enumerate(zip(sources, places))
    ]
    for copy in copies:
        copy.start()
    for copy in copies:
        copy.wait()
    length, width = inp_ref.shape
    states = rate_ref.shape[0]
    tiles = width // LANES
    for j in range(tiles):
        cols = slice(j * LANES, (j + 1) * LANES)
        pad_ref[SUB - KCONV + 1 : SUB, :] = before_ref[:, cols].astype(jnp.float32)
        pad_ref[SUB:, :] = inp_ref[:, cols].astype(jnp.float32)
        summed = jnp.broadcast_to(bias_ref[:, cols], (length, LANES))
        for k in range(KCONV):
            begin = SUB - KCONV + 1 + k
            summed = summed + taps_ref[k : k + 1, cols] * pad_ref[begin : begin + length, :]
        conv_ref[pl.ds(j, length, stride=tiles), :] = summed * jax.nn.sigmoid(summed)
        raw = raw_ref[:, cols].astype(jnp.float32)
        delta_ref[pl.ds(j, length, stride=tiles), :] = jnp.maximum(raw, 0.0) + jnp.log1p(
            jnp.exp(-jnp.abs(raw))
        )
        scaled_ref[pl.ds(j, states, stride=tiles), :] = rate_ref[:, cols] * -LOG2E

    skip = skip_ref[...]

    def step(t, carry):
        total, state = carry
        rows = pl.ds(pl.multiple_of(t * SUB, SUB), SUB)
        delta, value = delta_ref[rows, :], conv_ref[rows, :]
        total = total + delta
        out = skip * value
        after = []
        for n in range(states):
            retain = jnp.exp2(delta * scaled_ref[n * SUB : (n + 1) * SUB, :])
            fresh = in_ref[t * states + n] * value
            now = fresh + retain * (state[n] - fresh)
            out = out + out_ref[t * states + n] * now
            after.append(now)
        sums_ref[rows, :] = total
        y_ref[rows, :] = out
        return total, tuple(after)

    zero = jnp.zeros((SUB, LANES), jnp.float32)
    total, state = lax.fori_loop(0, length, step, (zero, (zero,) * states), unroll=2)
    for n in range(states):
        carry_ref[n * SUB : (n + 1) * SUB, :] = state[n]
    carry_ref[states * SUB :, :] = total


def finish_scan_kernel(
    y_ref, sums_ref, start_ref, scaled_ref, gate_hbm, out_ref, mixed_ref, full_ref, gate_ref, sem
):
    copy = pltpu.make_async_copy(gate_hbm, gate_ref, sem)
    copy.start()
    length, width = gate_ref.shape
    states = start_ref.shape[0] // SUB
    tiles = width // LANES

    def step(t, carry):
        rows = pl.ds(pl.multiple_of(t * SUB, SUB), SUB)
        total, out = sums_ref[rows, :], y_ref[rows, :]
        for n in range(states):
            part = slice(n * SUB, (n + 1) * SUB)
            kept = jnp.exp2(total * scaled_ref[part, :]) * start_ref[part, :]
            out = out + out_ref[t * states + n] * kept
        full_ref[rows, :] = out
        return carry

    lax.fori_loop(0, length, step, 0, unroll=2)
    copy.wait()
    for j in range(tiles):
        cols = slice(j * LANES, (j + 1) * LANES)
        gate = gate_ref[:, cols].astype(jnp.float32)
        gated = full_ref[pl.ds(j, length, stride=tiles), :] * (gate * jax.nn.sigmoid(gate))
        mixed_ref[:, cols] = gated.astype(mixed_ref.dtype)


def local_scan(inp, before, raw, rate, taps, bias, skip, in_flat, out_flat):
    length, width = inp.shape
    states = rate.shape[0]
    flat = jax.ShapeDtypeStruct((length * SUB, LANES), jnp.float32)
    arrays = (inp, raw, rate, taps, bias, skip)
    return pl.pallas_call(
        local_scan_kernel,
        name="local_scan",
        out_shape=(
            flat,
            flat,
            jax.ShapeDtypeStruct(((states + 1) * SUB, LANES), jnp.float32),
            jax.ShapeDtypeStruct((states * SUB, LANES), jnp.float32),
        ),
        in_specs=[HBM] * 6 + [VMEM] + [SMEM] * 2,
        out_specs=(VMEM,) * 4,
        scratch_shapes=[pltpu.VMEM(a.shape, a.dtype) for a in arrays]
        + [
            pltpu.VMEM((length + SUB, LANES), jnp.float32),
            pltpu.VMEM((length * SUB, LANES), jnp.float32),
            pltpu.VMEM((length * SUB, LANES), jnp.float32),
            pltpu.SemaphoreType.DMA((6,)),
        ],
        compiler_params=pltpu.CompilerParams(vmem_limit_bytes=58 << 20),
        cost_estimate=pl.CostEstimate(flops=8_000_000, transcendentals=2_500_000, bytes_accessed=2_000_000),
    )(*arrays, before, in_flat, out_flat)


def finish_scan(y, sums, start, scaled, gate, out_flat):
    length, width = gate.shape
    return pl.pallas_call(
        finish_scan_kernel,
        name="finish_scan",
        out_shape=jax.ShapeDtypeStruct((length, width), jnp.bfloat16),
        in_specs=[VMEM] * 4 + [HBM] + [SMEM],
        out_specs=VMEM,
        scratch_shapes=[
            pltpu.VMEM((length * SUB, LANES), jnp.float32),
            pltpu.VMEM((length, width), jnp.bfloat16),
            pltpu.SemaphoreType.DMA,
        ],
        compiler_params=pltpu.CompilerParams(vmem_limit_bytes=16 << 20),
        cost_estimate=pl.CostEstimate(flops=8_000_000, transcendentals=2_500_000, bytes_accessed=2_000_000),
    )(y, sums, start, scaled, gate, out_flat)


def entering_state(carry, scaled):
    states = scaled.shape[0] // SUB
    scaled = scaled.reshape(states, SUB, LANES)
    y, x, c = split_place(lax.axis_index("seq"))

    def parts(block):
        block = block.reshape(states + 1, SUB, LANES)
        return block[states], block[:states]

    def kept(span, state):
        return jnp.exp2(span[None] * scaled) * state

    def packed(span, state):
        return jnp.concatenate([state, span[None]], axis=0).reshape(carry.shape)

    own = parts(carry)
    other = parts(moved(carry, dc=1))
    is_first = c == 0
    first = [jnp.where(is_first, a, b) for a, b in zip(own, other)]
    last = [jnp.where(is_first, b, a) for a, b in zip(own, other)]
    chip = (first[0] + last[0], kept(last[0], first[1]) + last[1])
    start = jnp.where(is_first, 0.0, other[1])
    span = jnp.where(is_first, 0.0, other[0])

    sent = packed(*chip)
    near = [parts(moved(sent, dx=k)) for k in range(1, SIDE)]
    ahead = jnp.zeros_like(span)
    behind = jnp.zeros_like(span)
    row_state = jnp.zeros_like(chip[1])
    earlier_state = jnp.zeros_like(chip[1])
    for k in range(1, SIDE):
        got_span, got_state = near[k - 1]
        is_earlier = k <= x
        earlier_state = earlier_state + jnp.where(is_earlier, kept(ahead, got_state), 0.0)
        row_state = row_state + jnp.where(is_earlier, 0.0, kept(behind, got_state))
        ahead = ahead + jnp.where(is_earlier, got_span, 0.0)
        behind = behind + jnp.where(is_earlier, 0.0, got_span)
    row_state = row_state + kept(behind, chip[1] + kept(chip[0], earlier_state))
    row_span = ahead + chip[0] + behind
    start = start + kept(span, earlier_state)
    span = span + ahead

    sent = packed(row_span, row_state)
    far = [parts(moved(sent, dy=k)) for k in range(1, SIDE)]
    for k in range(1, SIDE):
        got_span, got_state = far[k - 1]
        is_earlier = k <= y
        start = start + jnp.where(is_earlier, kept(span, got_state), 0.0)
        span = span + jnp.where(is_earlier, got_span, 0.0)
    return start.reshape(states * SUB, LANES)


def from_before(tail):
    count = lax.axis_size("seq")
    return lax.ppermute(tail, "seq", [(i, i + 1) for i in range(count - 1)])


def around(block, ring, step):
    route = []
    for i in range(SIDE * SIDE * CORES):
        y, x, c = split_place(i)
        along_x = (ring == "inner") == (c == 0)
        dy, dx = (0, step) if along_x else (step, 0)
        route.append((i, join_place(y + dy, x + dx, c)))
    return lax.ppermute(block, "seq", route)


def added(*terms):
    return sum(t.astype(jnp.float32) for t in terms)


def expert_in_kernel(*refs):
    pieces, (gate_a, gate_b, up_a, up_b, act_a, act_b, rows_ref) = refs[:-7], refs[-7:]
    rows = pieces[0].shape[0]

    @pl.when(pl.program_id(0) == 0)
    def _():
        for k, piece in enumerate(pieces):
            rows_ref[k * rows : (k + 1) * rows, :] = piece[...]

    for gate, up, act in ((gate_a, up_a, act_a), (gate_b, up_b, act_b)):
        both = jnp.concatenate([gate[...], up[...]], axis=1)
        hidden = jnp.dot(rows_ref[...], both, preferred_element_type=jnp.float32)
        gating, upward = hidden[:, :LANES], hidden[:, LANES:]
        act[...] = (gating * jax.nn.sigmoid(gating) * upward).astype(act.dtype)


def expert_in(pieces, here, there):
    rows, width = pieces[0].shape
    count = len(pieces) * rows
    hidden = here[0].shape[1]
    weight = pl.BlockSpec((width, LANES), lambda i: (0, i))
    act = pl.BlockSpec((count, LANES), lambda i: (0, i))
    return pl.pallas_call(
        expert_in_kernel,
        name="expert_in",
        grid=(hidden // LANES,),
        out_shape=(jax.ShapeDtypeStruct((count, hidden), jnp.bfloat16),) * 2,
        in_specs=[VMEM] * len(pieces) + [weight] * 4,
        out_specs=(act, act),
        scratch_shapes=[pltpu.VMEM((count, width), jnp.bfloat16)],
        compiler_params=pltpu.CompilerParams(vmem_limit_bytes=50 << 20),
        cost_estimate=pl.CostEstimate(
            flops=8 * count * width * hidden, transcendentals=2 * count * hidden, bytes_accessed=16_000_000
        ),
    )(*pieces, here[0], there[0], here[1], there[1])


def expert_out_kernel(places, rows, *refs):
    acts, (down_a, down_b) = refs[:4], refs[4:6]
    outs, acts_ref = refs[6:-1], refs[-1]
    hidden = down_a.shape[0]

    @pl.when(pl.program_id(0) == 0)
    def _():
        for k, (part, begin) in enumerate(places):
            for side in range(2):
                block = acts[2 * part + side][begin * rows : (begin + 1) * rows, :]
                acts_ref[k * rows : (k + 1) * rows, side * hidden : (side + 1) * hidden] = block

    down = jnp.concatenate([down_a[...], down_b[...]], axis=0)
    result = jnp.dot(acts_ref[...], down, preferred_element_type=jnp.float32)
    for k, out in enumerate(outs):
        out[...] = result[k * rows : (k + 1) * rows].astype(out.dtype)


def expert_out(places, rows, acts, here, there):
    hidden, width = here[2].shape
    count = len(places) * rows
    tile = 8 * LANES
    weight = pl.BlockSpec((hidden, tile), lambda i: (0, i))
    piece = pl.BlockSpec((rows, tile), lambda i: (0, i))
    return pl.pallas_call(
        functools.partial(expert_out_kernel, places, rows),
        name="expert_out",
        grid=(width // tile,),
        out_shape=(jax.ShapeDtypeStruct((rows, width), jnp.bfloat16),) * len(places),
        in_specs=[VMEM] * 4 + [weight] * 2,
        out_specs=(piece,) * len(places),
        scratch_shapes=[pltpu.VMEM((count, 2 * hidden), jnp.bfloat16)],
        compiler_params=pltpu.CompilerParams(vmem_limit_bytes=50 << 20),
        cost_estimate=pl.CostEstimate(
            flops=4 * count * width * hidden, transcendentals=0, bytes_accessed=9_000_000
        ),
    )(*acts, here[2], there[2])


def experts_of_rows(block, here, there):
    dtype = block.dtype
    half = block.shape[1] // 2
    after, before = around(block, "inner", 1), around(block, "inner", -1)
    across = jnp.concatenate(
        [around(after[:, :half], "inner", 1), around(before[:, half:], "inner", -1)], axis=1
    )
    near = [block, after, across, before]
    low, high = jnp.concatenate(near[:2], axis=0), jnp.concatenate(near[2:], axis=0)
    low_up = around(low, "outer", 1)
    high_down = around(high, "outer", -1)
    high_up = around(high, "outer", 1)
    low_down = around(low, "outer", -1)
    low_far = around(low_up, "outer", 1)
    high_far = around(high_down, "outer", -1)
    acts = expert_in([low, high, low_up, high_down], here, there)
    acts = [*acts, *expert_in([low_far, high_far, low_down, high_up], here, there)]
    rows = low.shape[0]
    low_far, high_far, low_up, high_down = expert_out(((1, 0), (1, 1), (0, 2), (0, 3)), rows, acts, here, there)
    got_high_down = around(high_down, "outer", 1)
    got_low_up = around(low_up, "outer", -1)
    low, high, low_down, high_up = expert_out(((0, 0), (0, 1), (1, 2), (1, 3)), rows, acts, here, there)
    low_relay = around(low_far, "outer", 1)
    high_relay = around(high_far, "outer", -1)
    got_low_down = around(added(low_down, low_relay).astype(dtype), "outer", 1)
    got_high_up = around(added(high_up, high_relay).astype(dtype), "outer", -1)
    low_sum = added(low, got_low_up, got_low_down)
    high_sum = added(high, got_high_down, got_high_up)
    rows = block.shape[0]
    blocks = [low_sum[:rows], low_sum[rows:], high_sum[:rows], high_sum[rows:]]
    back = [around(blocks[k].astype(dtype), "inner", -k) for k in range(1, SIDE)]
    return added(blocks[0], *back).astype(dtype)


def project_kernel(mixed_ref, *refs):
    blocks, out_ref = refs[:-1], refs[-1]
    owners, rows = out_ref.shape[:2]
    weight = jnp.concatenate([block[...] for block in blocks], axis=1)
    result = jnp.dot(mixed_ref[...], weight, preferred_element_type=jnp.float32).astype(out_ref.dtype)
    for owner in range(owners):
        out_ref[owner] = result[owner * rows : (owner + 1) * rows]


def project(mixed, weight):
    blocks = lax.all_gather(weight, "seq")
    owners = lax.axis_size("exp")
    tokens, depth = mixed.shape
    count = blocks.shape[0]
    group = SIDE
    rows = tokens // owners
    views = [pl.BlockSpec((None, depth, LANES), lambda i, q=q: (group * i + q, 0, 0)) for q in range(group)]
    terms = pl.pallas_call(
        project_kernel,
        name="project",
        grid=(count // group,),
        out_shape=jax.ShapeDtypeStruct((owners, rows, count * LANES), jnp.bfloat16),
        in_specs=[VMEM] + views,
        out_specs=pl.BlockSpec((owners, rows, group * LANES), lambda i: (0, 0, i)),
        compiler_params=pltpu.CompilerParams(vmem_limit_bytes=56 << 20),
        cost_estimate=pl.CostEstimate(
            flops=2 * tokens * depth * count * LANES, transcendentals=0, bytes_accessed=10_000_000
        ),
    )(mixed, *([blocks] * group))
    terms = lax.all_to_all(terms, "exp", 0, 0, tiled=True)
    return added(*(terms[k] for k in range(owners)))


def shards(
    mixer_input,
    gate_input,
    delta_raw,
    input_coef,
    output_coef,
    decay_rate,
    conv_weight,
    conv_bias,
    skip_gain,
    out_weight,
    residual,
    norm_gain,
    router_weight,
    expert_ids,
    gate_weight,
    up_weight,
    down_weight,
):
    length = mixer_input.shape[0]
    in_flat = input_coef.astype(jnp.float32).reshape(-1)
    out_flat = output_coef.astype(jnp.float32).reshape(-1)
    before = from_before(mixer_input[length - (KCONV - 1) :])
    y, sums, carry, scaled = local_scan(
        mixer_input,
        before,
        delta_raw,
        decay_rate,
        conv_weight,
        conv_bias.reshape(1, -1),
        skip_gain.reshape(SUB, LANES),
        in_flat,
        out_flat,
    )
    here = [w[0] for w in (gate_weight, up_weight, down_weight)]
    there = [moved(w, dc=1) for w in here]
    carry, *there = lax.optimization_barrier((carry, *there))
    start = entering_state(carry, scaled)
    mixed = finish_scan(y, sums, start, scaled, gate_input, out_flat)
    rows = residual.shape[0]
    model_width = residual.shape[1]
    projected = project(mixed, out_weight)
    hidden_state = residual.astype(jnp.float32) + projected
    scale = lax.rsqrt(jnp.mean(hidden_state * hidden_state, axis=1, keepdims=True) + 1e-06)
    normed = (hidden_state * scale * norm_gain[None, :]).astype(jnp.bfloat16)
    experts = router_weight.shape[1]
    capacity = 2 * rows // experts + 1
    logits = jnp.dot(normed, router_weight, preferred_element_type=jnp.float32)
    expert_range = jnp.arange(experts, dtype=jnp.int32)
    matches = expert_ids[:, :, None] == expert_range[None, None, :]
    chosen = jnp.sum(jnp.where(matches, logits[:, None, :], 0.0), axis=2)
    first = jax.nn.sigmoid(chosen[:, 0] - chosen[:, 1])
    flat_ids = expert_ids.reshape(-1)
    position = jnp.arange(flat_ids.shape[0], dtype=jnp.int32)
    earlier = (flat_ids[:, None] == flat_ids[None, :]) & (position[None, :] < position[:, None])
    rank = jnp.sum(earlier.astype(jnp.int32), axis=1)
    target = flat_ids * capacity + rank
    placing = (jnp.arange(experts * capacity, dtype=jnp.int32)[:, None] == target[None, :]).astype(
        jnp.bfloat16
    )
    repeated = jnp.broadcast_to(normed[:, None, :], (rows, 2, model_width)).reshape(-1, model_width)
    outgoing = jnp.dot(placing, repeated, preferred_element_type=jnp.float32).astype(jnp.bfloat16)
    outgoing = outgoing.reshape(experts, -1, LANES)
    arrived = lax.all_to_all(outgoing, "exp", split_axis=0, concat_axis=0, tiled=True)
    flat_rows = arrived.reshape(-1, model_width)
    summed_out = experts_of_rows(flat_rows, here, there)
    returned = lax.all_to_all(
        summed_out.reshape(arrived.shape), "exp", split_axis=0, concat_axis=0, tiled=True
    )
    flat_returned = returned.reshape(-1, model_width)
    picked = jnp.einsum(
        "sa,sd->ad", placing, flat_returned, preferred_element_type=jnp.float32
    ).reshape(rows, 2, model_width)
    moe_out = first[:, None] * picked[:, 0] + (1.0 - first)[:, None] * picked[:, 1]
    final = (hidden_state + moe_out).astype(jnp.bfloat16)
    return (mixed, final)


def solution(mesh):
    return jax.shard_map(
        shards,
        mesh=mesh,
        in_specs=(
            P("seq", "exp"),
            P("seq", "exp"),
            P("seq", "exp"),
            P("seq", None),
            P("seq", None),
            P(None, "exp"),
            P(None, "exp"),
            P("exp"),
            P("exp"),
            P("exp", "seq"),
            P(("seq", "exp"), None),
            P(),
            P(),
            P(("seq", "exp"), None),
            P("exp", None, "seq"),
            P("exp", None, "seq"),
            P("exp", "seq", None),
        ),
        out_specs=(P("seq", "exp"), P(("seq", "exp"), None)),
        check_vma=False,
    )
```

```python
import functools
import math

import jax
import jax.numpy as jnp
from jax import lax
from jax.experimental import pallas as pl
from jax.experimental.pallas import tpu as pltpu
from jax.sharding import PartitionSpec as P

KCONV = 4
LANES = 128
SUB = 8
CORES = 2
SIDE = 4
LOG2E = math.log2(math.e)
VMEM = pl.BlockSpec(memory_space=pltpu.VMEM)
SMEM = pl.BlockSpec(memory_space=pltpu.SMEM)
HBM = pl.BlockSpec(memory_space=pltpu.MemorySpace.HBM)


def split_place(place):
    return place // (SIDE * CORES), (place // CORES) % SIDE, place % CORES


def join_place(y, x, c):
    return (y % SIDE * SIDE + x % SIDE) * CORES + c % CORES


def moved(block, dy=0, dx=0, dc=0):
    route = []
    for i in range(SIDE * SIDE * CORES):
        y, x, c = split_place(i)
        route.append((i, join_place(y + dy, x + dx, c + dc)))
    return lax.ppermute(block, "seq", route)


def local_scan_kernel(
    inp_hbm, raw_hbm, rate_hbm, taps_hbm, bias_hbm, skip_hbm, before_ref, in_ref, out_ref,
    y_ref, sums_ref, carry_ref, scaled_ref,
    inp_ref, raw_ref, rate_ref, taps_ref, bias_ref, skip_ref, pad_ref, delta_ref, conv_ref, sems,
):
    sources = (inp_hbm, raw_hbm, rate_hbm, taps_hbm, bias_hbm, skip_hbm)
    places = (inp_ref, raw_ref, rate_ref, taps_ref, bias_ref, skip_ref)
    copies = [
        pltpu.make_async_copy(source, place, sems.at[k])
        for k, (source, place) in enumerate(zip(sources, places))
    ]
    for copy in copies:
        copy.start()
    for copy in copies:
        copy.wait()
    length, width = inp_ref.shape
    states = rate_ref.shape[0]
    tiles = width // LANES
    for j in range(tiles):
        cols = slice(j * LANES, (j + 1) * LANES)
        pad_ref[SUB - KCONV + 1 : SUB, :] = before_ref[:, cols].astype(jnp.float32)
        pad_ref[SUB:, :] = inp_ref[:, cols].astype(jnp.float32)
        summed = jnp.broadcast_to(bias_ref[:, cols], (length, LANES))
        for k in range(KCONV):
            begin = SUB - KCONV + 1 + k
            summed = summed + taps_ref[k : k + 1, cols] * pad_ref[begin : begin + length, :]
        conv_ref[pl.ds(j, length, stride=tiles), :] = summed * jax.nn.sigmoid(summed)
        raw = raw_ref[:, cols].astype(jnp.float32)
        delta_ref[pl.ds(j, length, stride=tiles), :] = jnp.maximum(raw, 0.0) + jnp.log1p(
            jnp.exp(-jnp.abs(raw))
        )
        scaled_ref[pl.ds(j, states, stride=tiles), :] = rate_ref[:, cols] * -LOG2E

    skip = skip_ref[...]

    def step(t, carry):
        total, state = carry
        rows = pl.ds(pl.multiple_of(t * SUB, SUB), SUB)
        delta, value = delta_ref[rows, :], conv_ref[rows, :]
        total = total + delta
        out = skip * value
        after = []
        for n in range(states):
            retain = jnp.exp2(delta * scaled_ref[n * SUB : (n + 1) * SUB, :])
            fresh = in_ref[t * states + n] * value
            now = fresh + retain * (state[n] - fresh)
            out = out + out_ref[t * states + n] * now
            after.append(now)
        sums_ref[rows, :] = total
        y_ref[rows, :] = out
        return total, tuple(after)

    zero = jnp.zeros((SUB, LANES), jnp.float32)
    total, state = lax.fori_loop(0, length, step, (zero, (zero,) * states), unroll=2)
    for n in range(states):
        carry_ref[n * SUB : (n + 1) * SUB, :] = state[n]
    carry_ref[states * SUB :, :] = total


def finish_scan_kernel(
    y_ref, sums_ref, start_ref, scaled_ref, gate_hbm, out_ref, mixed_ref, full_ref, gate_ref, sem
):
    copy = pltpu.make_async_copy(gate_hbm, gate_ref, sem)
    copy.start()
    length, width = gate_ref.shape
    states = start_ref.shape[0] // SUB
    tiles = width // LANES

    def step(t, carry):
        rows = pl.ds(pl.multiple_of(t * SUB, SUB), SUB)
        total, out = sums_ref[rows, :], y_ref[rows, :]
        for n in range(states):
            part = slice(n * SUB, (n + 1) * SUB)
            kept = jnp.exp2(total * scaled_ref[part, :]) * start_ref[part, :]
            out = out + out_ref[t * states + n] * kept
        full_ref[rows, :] = out
        return carry

    lax.fori_loop(0, length, step, 0, unroll=2)
    copy.wait()
    for j in range(tiles):
        cols = slice(j * LANES, (j + 1) * LANES)
        gate = gate_ref[:, cols].astype(jnp.float32)
        gated = full_ref[pl.ds(j, length, stride=tiles), :] * (gate * jax.nn.sigmoid(gate))
        mixed_ref[:, cols] = gated.astype(mixed_ref.dtype)


def local_scan(inp, before, raw, rate, taps, bias, skip, in_flat, out_flat):
    length, width = inp.shape
    states = rate.shape[0]
    flat = jax.ShapeDtypeStruct((length * SUB, LANES), jnp.float32)
    arrays = (inp, raw, rate, taps, bias, skip)
    return pl.pallas_call(
        local_scan_kernel,
        name="local_scan",
        out_shape=(
            flat,
            flat,
            jax.ShapeDtypeStruct(((states + 1) * SUB, LANES), jnp.float32),
            jax.ShapeDtypeStruct((states * SUB, LANES), jnp.float32),
        ),
        in_specs=[HBM] * 6 + [VMEM] + [SMEM] * 2,
        out_specs=(VMEM,) * 4,
        scratch_shapes=[pltpu.VMEM(a.shape, a.dtype) for a in arrays]
        + [
            pltpu.VMEM((length + SUB, LANES), jnp.float32),
            pltpu.VMEM((length * SUB, LANES), jnp.float32),
            pltpu.VMEM((length * SUB, LANES), jnp.float32),
            pltpu.SemaphoreType.DMA((6,)),
        ],
        compiler_params=pltpu.CompilerParams(vmem_limit_bytes=58 << 20),
        cost_estimate=pl.CostEstimate(flops=8_000_000, transcendentals=2_500_000, bytes_accessed=2_000_000),
    )(*arrays, before, in_flat, out_flat)


def finish_scan(y, sums, start, scaled, gate, out_flat):
    length, width = gate.shape
    return pl.pallas_call(
        finish_scan_kernel,
        name="finish_scan",
        out_shape=jax.ShapeDtypeStruct((length, width), jnp.bfloat16),
        in_specs=[VMEM] * 4 + [HBM] + [SMEM],
        out_specs=VMEM,
        scratch_shapes=[
            pltpu.VMEM((length * SUB, LANES), jnp.float32),
            pltpu.VMEM((length, width), jnp.bfloat16),
            pltpu.SemaphoreType.DMA,
        ],
        compiler_params=pltpu.CompilerParams(vmem_limit_bytes=16 << 20),
        cost_estimate=pl.CostEstimate(flops=8_000_000, transcendentals=2_500_000, bytes_accessed=2_000_000),
    )(y, sums, start, scaled, gate, out_flat)


def entering_state(carry, scaled):
    states = scaled.shape[0] // SUB
    scaled = scaled.reshape(states, SUB, LANES)
    y, x, c = split_place(lax.axis_index("seq"))

    def parts(block):
        block = block.reshape(states + 1, SUB, LANES)
        return block[states], block[:states]

    def kept(span, state):
        return jnp.exp2(span[None] * scaled) * state

    def packed(span, state):
        return jnp.concatenate([state, span[None]], axis=0).reshape(carry.shape)

    own = parts(carry)
    other = parts(moved(carry, dc=1))
    is_first = c == 0
    first = [jnp.where(is_first, a, b) for a, b in zip(own, other)]
    last = [jnp.where(is_first, b, a) for a, b in zip(own, other)]
    chip = (first[0] + last[0], kept(last[0], first[1]) + last[1])
    start = jnp.where(is_first, 0.0, other[1])
    span = jnp.where(is_first, 0.0, other[0])

    sent = packed(*chip)
    near = [parts(moved(sent, dx=k)) for k in range(1, SIDE)]
    ahead = jnp.zeros_like(span)
    behind = jnp.zeros_like(span)
    row_state = jnp.zeros_like(chip[1])
    earlier_state = jnp.zeros_like(chip[1])
    for k in range(1, SIDE):
        got_span, got_state = near[k - 1]
        is_earlier = k <= x
        earlier_state = earlier_state + jnp.where(is_earlier, kept(ahead, got_state), 0.0)
        row_state = row_state + jnp.where(is_earlier, 0.0, kept(behind, got_state))
        ahead = ahead + jnp.where(is_earlier, got_span, 0.0)
        behind = behind + jnp.where(is_earlier, 0.0, got_span)
    row_state = row_state + kept(behind, chip[1] + kept(chip[0], earlier_state))
    row_span = ahead + chip[0] + behind
    start = start + kept(span, earlier_state)
    span = span + ahead

    sent = packed(row_span, row_state)
    far = [parts(moved(sent, dy=k)) for k in range(1, SIDE)]
    for k in range(1, SIDE):
        got_span, got_state = far[k - 1]
        is_earlier = k <= y
        start = start + jnp.where(is_earlier, kept(span, got_state), 0.0)
        span = span + jnp.where(is_earlier, got_span, 0.0)
    return start.reshape(states * SUB, LANES)


def from_before(tail):
    count = lax.axis_size("seq")
    return lax.ppermute(tail, "seq", [(i, i + 1) for i in range(count - 1)])


def around(block, ring, step):
    route = []
    for i in range(SIDE * SIDE * CORES):
        y, x, c = split_place(i)
        along_x = (ring == "inner") == (c == 0)
        dy, dx = (0, step) if along_x else (step, 0)
        route.append((i, join_place(y + dy, x + dx, c)))
    return lax.ppermute(block, "seq", route)


def added(*terms):
    return sum(t.astype(jnp.float32) for t in terms)


def expert_in_kernel(*refs):
    pieces, (gate_a, gate_b, up_a, up_b, act_a, act_b, rows_ref) = refs[:-7], refs[-7:]
    rows = pieces[0].shape[0]

    @pl.when(pl.program_id(0) == 0)
    def _():
        for k, piece in enumerate(pieces):
            rows_ref[k * rows : (k + 1) * rows, :] = piece[...]

    for gate, up, act in ((gate_a, up_a, act_a), (gate_b, up_b, act_b)):
        both = jnp.concatenate([gate[...], up[...]], axis=1)
        hidden = jnp.dot(rows_ref[...], both, preferred_element_type=jnp.float32)
        gating, upward = hidden[:, :LANES], hidden[:, LANES:]
        act[...] = (gating * jax.nn.sigmoid(gating) * upward).astype(act.dtype)


def expert_in(pieces, here, there):
    rows, width = pieces[0].shape
    count = len(pieces) * rows
    hidden = here[0].shape[1]
    weight = pl.BlockSpec((width, LANES), lambda i: (0, i))
    act = pl.BlockSpec((count, LANES), lambda i: (0, i))
    return pl.pallas_call(
        expert_in_kernel,
        name="expert_in",
        grid=(hidden // LANES,),
        out_shape=(jax.ShapeDtypeStruct((count, hidden), jnp.bfloat16),) * 2,
        in_specs=[VMEM] * len(pieces) + [weight] * 4,
        out_specs=(act, act),
        scratch_shapes=[pltpu.VMEM((count, width), jnp.bfloat16)],
        compiler_params=pltpu.CompilerParams(vmem_limit_bytes=50 << 20),
        cost_estimate=pl.CostEstimate(
            flops=8 * count * width * hidden, transcendentals=2 * count * hidden, bytes_accessed=16_000_000
        ),
    )(*pieces, here[0], there[0], here[1], there[1])


def expert_out_kernel(places, rows, *refs):
    acts, downs = refs[:4], refs[4:8]
    outs, acts_ref = refs[8:-1], refs[-1]
    hidden = acts_ref.shape[1] // 2

    @pl.when(pl.program_id(0) == 0)
    def _():
        for k, (part, begin) in enumerate(places):
            for side in range(2):
                block = acts[2 * part + side][begin * rows : (begin + 1) * rows, :]
                acts_ref[k * rows : (k + 1) * rows, side * hidden : (side + 1) * hidden] = block

    down = jnp.concatenate([d[...] for d in downs], axis=0)
    result = jnp.dot(acts_ref[...], down, preferred_element_type=jnp.float32)
    for k, out in enumerate(outs):
        out[...] = result[k * rows : (k + 1) * rows].astype(out.dtype)


def expert_out(places, rows, acts, here, there):
    hidden, width = here[2].shape
    count = len(places) * rows
    tile = 8 * LANES
    weights = [pl.BlockSpec((hidden // 2, tile), lambda i, h=h: (h, i)) for h in range(2)]
    piece = pl.BlockSpec((rows, tile), lambda i: (0, i))
    return pl.pallas_call(
        functools.partial(expert_out_kernel, places, rows),
        name="expert_out",
        grid=(width // tile,),
        out_shape=(jax.ShapeDtypeStruct((rows, width), jnp.bfloat16),) * len(places),
        in_specs=[VMEM] * 4 + weights * 2,
        out_specs=(piece,) * len(places),
        scratch_shapes=[pltpu.VMEM((count, 2 * hidden), jnp.bfloat16)],
        compiler_params=pltpu.CompilerParams(vmem_limit_bytes=50 << 20),
        cost_estimate=pl.CostEstimate(
            flops=4 * count * width * hidden, transcendentals=0, bytes_accessed=9_000_000
        ),
    )(*acts, here[2], here[2], there[2], there[2])


def experts_of_rows(block, here, there):
    dtype = block.dtype
    half = block.shape[1] // 2
    after, before = around(block, "inner", 1), around(block, "inner", -1)
    across = jnp.concatenate(
        [around(after[:, :half], "inner", 1), around(before[:, half:], "inner", -1)], axis=1
    )
    near = [block, after, across, before]
    low, high = jnp.concatenate(near[:2], axis=0), jnp.concatenate(near[2:], axis=0)
    low_up = around(low, "outer", 1)
    high_down = around(high, "outer", -1)
    high_up = around(high, "outer", 1)
    low_down = around(low, "outer", -1)
    low_far = around(low_up, "outer", 1)
    high_far = around(high_down, "outer", -1)
    acts = expert_in([low, high, low_up, high_down], here, there)
    acts = [*acts, *expert_in([low_far, high_far, low_down, high_up], here, there)]
    rows = low.shape[0]
    low_far, high_far, low_up, high_down = expert_out(((1, 0), (1, 1), (0, 2), (0, 3)), rows, acts, here, there)
    got_high_down = around(high_down, "outer", 1)
    got_low_up = around(low_up, "outer", -1)
    low, high, low_down, high_up = expert_out(((0, 0), (0, 1), (1, 2), (1, 3)), rows, acts, here, there)
    low_relay = around(low_far, "outer", 1)
    high_relay = around(high_far, "outer", -1)
    got_low_down = around(added(low_down, low_relay).astype(dtype), "outer", 1)
    got_high_up = around(added(high_up, high_relay).astype(dtype), "outer", -1)
    low_sum = added(low, got_low_up, got_low_down)
    high_sum = added(high, got_high_down, got_high_up)
    rows = block.shape[0]
    blocks = [low_sum[:rows], low_sum[rows:], high_sum[:rows], high_sum[rows:]]
    back = [around(blocks[k].astype(dtype), "inner", -k) for k in range(1, SIDE)]
    return added(blocks[0], *back).astype(dtype)


def project_kernel(mixed_ref, *refs):
    blocks, out_ref = refs[:-1], refs[-1]
    owners, rows = out_ref.shape[:2]
    weight = jnp.concatenate([block[...] for block in blocks], axis=1)
    result = jnp.dot(mixed_ref[...], weight, preferred_element_type=jnp.float32).astype(out_ref.dtype)
    for owner in range(owners):
        out_ref[owner] = result[owner * rows : (owner + 1) * rows]


def project(mixed, weight):
    blocks = lax.all_gather(weight, "seq")
    owners = lax.axis_size("exp")
    tokens, depth = mixed.shape
    count = blocks.shape[0]
    group = 2 * SIDE
    rows = tokens // owners
    views = [pl.BlockSpec((None, depth, LANES), lambda i, q=q: (group * i + q, 0, 0)) for q in range(group)]
    terms = pl.pallas_call(
        project_kernel,
        name="project",
        grid=(count // group,),
        out_shape=jax.ShapeDtypeStruct((owners, rows, count * LANES), jnp.bfloat16),
        in_specs=[VMEM] + views,
        out_specs=pl.BlockSpec((owners, rows, group * LANES), lambda i: (0, 0, i)),
        compiler_params=pltpu.CompilerParams(vmem_limit_bytes=56 << 20),
        cost_estimate=pl.CostEstimate(
            flops=2 * tokens * depth * count * LANES, transcendentals=0, bytes_accessed=10_000_000
        ),
    )(mixed, *([blocks] * group))
    terms = lax.all_to_all(terms, "exp", 0, 0, tiled=True)
    return added(*(terms[k] for k in range(owners)))


def shards(
    mixer_input,
    gate_input,
    delta_raw,
    input_coef,
    output_coef,
    decay_rate,
    conv_weight,
    conv_bias,
    skip_gain,
    out_weight,
    residual,
    norm_gain,
    router_weight,
    expert_ids,
    gate_weight,
    up_weight,
    down_weight,
):
    length = mixer_input.shape[0]
    in_flat = input_coef.astype(jnp.float32).reshape(-1)
    out_flat = output_coef.astype(jnp.float32).reshape(-1)
    before = from_before(mixer_input[length - (KCONV - 1) :])
    y, sums, carry, scaled = local_scan(
        mixer_input,
        before,
        delta_raw,
        decay_rate,
        conv_weight,
        conv_bias.reshape(1, -1),
        skip_gain.reshape(SUB, LANES),
        in_flat,
        out_flat,
    )
    here = [w[0] for w in (gate_weight, up_weight, down_weight)]
    there = [moved(w, dc=1) for w in here]
    carry, *there = lax.optimization_barrier((carry, *there))
    start = entering_state(carry, scaled)
    mixed = finish_scan(y, sums, start, scaled, gate_input, out_flat)
    rows = residual.shape[0]
    model_width = residual.shape[1]
    projected = project(mixed, out_weight)
    hidden_state = residual.astype(jnp.float32) + projected
    scale = lax.rsqrt(jnp.mean(hidden_state * hidden_state, axis=1, keepdims=True) + 1e-06)
    normed = (hidden_state * scale * norm_gain[None, :]).astype(jnp.bfloat16)
    experts = router_weight.shape[1]
    capacity = 2 * rows // experts + 1
    logits = jnp.dot(normed, router_weight, preferred_element_type=jnp.float32)
    expert_range = jnp.arange(experts, dtype=jnp.int32)
    matches = expert_ids[:, :, None] == expert_range[None, None, :]
    chosen = jnp.sum(jnp.where(matches, logits[:, None, :], 0.0), axis=2)
    first = jax.nn.sigmoid(chosen[:, 0] - chosen[:, 1])
    flat_ids = expert_ids.reshape(-1)
    position = jnp.arange(flat_ids.shape[0], dtype=jnp.int32)
    earlier = (flat_ids[:, None] == flat_ids[None, :]) & (position[None, :] < position[:, None])
    rank = jnp.sum(earlier.astype(jnp.int32), axis=1)
    target = flat_ids * capacity + rank
    placing = (jnp.arange(experts * capacity, dtype=jnp.int32)[:, None] == target[None, :]).astype(
        jnp.bfloat16
    )
    repeated = jnp.broadcast_to(normed[:, None, :], (rows, 2, model_width)).reshape(-1, model_width)
    outgoing = jnp.dot(placing, repeated, preferred_element_type=jnp.float32).astype(jnp.bfloat16)
    outgoing = outgoing.reshape(experts, -1, LANES)
    arrived = lax.all_to_all(outgoing, "exp", split_axis=0, concat_axis=0, tiled=True)
    flat_rows = arrived.reshape(-1, model_width)
    summed_out = experts_of_rows(flat_rows, here, there)
    returned = lax.all_to_all(
        summed_out.reshape(arrived.shape), "exp", split_axis=0, concat_axis=0, tiled=True
    )
    flat_returned = returned.reshape(-1, model_width)
    picked = jnp.einsum(
        "sa,sd->ad", placing, flat_returned, preferred_element_type=jnp.float32
    ).reshape(rows, 2, model_width)
    moe_out = first[:, None] * picked[:, 0] + (1.0 - first)[:, None] * picked[:, 1]
    final = (hidden_state + moe_out).astype(jnp.bfloat16)
    return (mixed, final)


def solution(mesh):
    return jax.shard_map(
        shards,
        mesh=mesh,
        in_specs=(
            P("seq", "exp"),
            P("seq", "exp"),
            P("seq", "exp"),
            P("seq", None),
            P("seq", None),
            P(None, "exp"),
            P(None, "exp"),
            P("exp"),
            P("exp"),
            P("exp", "seq"),
            P(("seq", "exp"), None),
            P(),
            P(),
            P(("seq", "exp"), None),
            P("exp", None, "seq"),
            P("exp", None, "seq"),
            P("exp", "seq", None),
        ),
        out_specs=(P("seq", "exp"), P(("seq", "exp"), None)),
        check_vma=False,
    )
```
